256 devices in a mesh: slab: 8 (over z), tile: 16 (over y, x), ch: 2 (over core).
Axes of the slice: x: 4, y: 4, z: 8, core: 2. Of those that a mesh axis runs over, the one named last changes fastest.
Arguments:
- volume: bfloat16 [16, 256, 1024], P('slab', 'tile'), may hold values from -6 to 6
- xz_tissue: int32 [256], P('tile'), may hold values 0 or 1
- yz_tissue: int32 [1024], P(('slab', 'tile')), may hold values 0 or 1
- first_conv: bfloat16 [32, 9, 1], replicated, may hold values from -2 to 2
- second_conv: bfloat16 [32, 9, 32], replicated, may hold values from -0.375 to 0.375
- third_conv: bfloat16 [64, 9, 32], replicated, may hold values from -0.375 to 0.375
- fourth_conv: bfloat16 [64, 9, 64], replicated, may hold values from -0.25 to 0.25
- fifth_conv: bfloat16 [32, 9, 96], replicated, may hold values from -0.21875 to 0.21875
- sixth_conv: bfloat16 [32, 9, 32], replicated, may hold values from -0.375 to 0.375
- out_weight: bfloat16 [32], replicated, may hold values from -1 to 1
Outputs:
- restored: bfloat16 [16, 256, 1024], P('slab', 'tile')
The draws below stay inside these ranges and needn't reach their ends.
All inputs are finite; a program needn't handle non-finite values. No bound on the sum of `xz_tissue` or of `yz_tissue` on one device may be relied on, other than what follows from the above.
Results may differ from the reference program's by a relative error of at most 0.0037.
Values may be sent and summed in bfloat16 or wider, within the bound.
No kernel may reach another device: no remote copies, remote signals or barrier semaphores. Data moves between devices by JAX's collectives and lax.ppermute only.
A program may use at most 128 MiB of HBM per device.

```python
import jax
import jax.numpy as jnp
from jax import lax

C1 = 32
C2 = 64
X = 1024
Z = 16
Y = 256


def plant(array, own_key, smallest, high):
    longest = array.shape.index(max(array.shape))
    spots = []
    for shift in (0, 1):
        where = [jax.random.randint(jax.random.fold_in(own_key, axis), (), 0, length) for axis, length in enumerate(array.shape)]
        where[longest] = (where[longest] + shift) % array.shape[longest]
        spots.append(tuple(where))
    return array.at[spots[0]].set(smallest).at[spots[1]].set(high)


def levels(own_key, extent, shards, smallest, top_value):
    factor_of = 1.0
    for dim, blocks in shards:
        draws = jax.random.uniform(jax.random.fold_in(jax.random.fold_in(own_key, 6), dim), (blocks,), jnp.float32, smallest / len(shards), top_value / len(shards))
        factor_of = factor_of * jnp.repeat(jnp.exp(draws), extent[dim] // blocks).reshape((-1,) + (1,) * (len(extent) - 1 - dim))
    return factor_of


def gaussian(stream_key, extent, width, most, split=(), held_as=jnp.bfloat16):
    loudness = levels(stream_key, extent, split, -0.22, 0.18) if split else 1.0
    drawn = jax.random.normal(stream_key, extent, jnp.float32) * width * loudness
    return jnp.minimum(jnp.maximum(drawn, -most), most).astype(held_as)


def setup_inputs(seed: int = 0) -> dict:
    splits = jax.random.split(jax.random.key(seed), 11)
    volume = gaussian(splits[0], (Z, Y, X), 1.0, 6.0, ((0, 8), (1, 16)))
    xz_tissue = plant((jax.random.randint(splits[1], (Y,), 0, 2) < 1).astype(jnp.int32), jax.random.fold_in(splits[1], 1), 0, 1)
    yz_tissue = plant((jax.random.randint(splits[2], (X,), 0, 2) < 1).astype(jnp.int32), jax.random.fold_in(splits[2], 1), 0, 1)
    first_conv = gaussian(splits[3], (C1, 9, 1), 9 ** -0.5, 2.0)
    second_conv = gaussian(splits[4], (C1, 9, C1), (9 * C1) ** -0.5, 0.375)
    third_conv = gaussian(splits[5], (C2, 9, C1), (9 * C1) ** -0.5, 0.375)
    fourth_conv = gaussian(splits[6], (C2, 9, C2), (9 * C2) ** -0.5, 0.25)
    fifth_conv = gaussian(splits[7], (C1, 9, C2 + C1), (9 * (C2 + C1)) ** -0.5, 0.21875)
    sixth_conv = gaussian(splits[8], (C1, 9, C1), (9 * C1) ** -0.5, 0.375)
    out_weight = gaussian(splits[9], (C1,), C1 ** -0.5, 1.0)
    return {"volume": volume, "xz_tissue": xz_tissue, "yz_tissue": yz_tissue, "first_conv": first_conv, "second_conv": second_conv, "third_conv": third_conv, "fourth_conv": fourth_conv, "fifth_conv": fifth_conv, "sixth_conv": sixth_conv, "out_weight": out_weight}


def convolve(signal, weight):
    channels, height, breadth = signal.shape
    padded = jnp.pad(signal, ((0, 0), (1, 1), (1, 1)))
    stacked = jnp.stack([padded[:, row_shift:row_shift + height, col_shift:col_shift + breadth] for row_shift in range(3) for col_shift in range(3)], axis=0)
    stacked = stacked.reshape(9 * channels, height, breadth).astype(jnp.float32)
    matrix = weight.reshape(weight.shape[0], 9 * channels).astype(jnp.float32)
    return jnp.einsum("ok,khw->ohw", matrix, stacked)


def activate(signal, weight):
    return jax.nn.relu(convolve(signal, weight)).astype(jnp.bfloat16)


def shrink(signal):
    channels, height, breadth = signal.shape
    blocks = signal.astype(jnp.float32).reshape(channels, height // 2, 2, breadth // 2, 2)
    return jnp.mean(blocks, axis=(2, 4)).astype(jnp.bfloat16)


def enlarge(signal):
    return jnp.repeat(jnp.repeat(signal, 2, axis=1), 2, axis=2)


def network(picture, weights):
    first_conv, second_conv, third_conv, fourth_conv, fifth_conv, sixth_conv, out_weight = weights
    opening = activate(picture[None], first_conv)
    skipped = activate(opening, second_conv)
    coarse = activate(shrink(skipped), third_conv)
    coarse = activate(coarse, fourth_conv)
    joined = jnp.concatenate([enlarge(coarse), skipped], axis=0)
    refined = activate(joined, fifth_conv)
    refined = activate(refined, sixth_conv)
    head = jnp.einsum("c,chw->hw", out_weight.astype(jnp.float32), refined.astype(jnp.float32))
    return picture.astype(jnp.float32) + head


def restore(planes, tissue, weights):
    def single(entry):
        picture, marker = entry
        value_new = network(picture, weights)
        return jnp.where(marker > 0, value_new, picture.astype(jnp.float32)).astype(jnp.bfloat16)

    return lax.map(single, (planes, tissue))


def reference(volume, xz_tissue, yz_tissue, first_conv, second_conv, third_conv, fourth_conv, fifth_conv, sixth_conv, out_weight):
    weights = (first_conv, second_conv, third_conv, fourth_conv, fifth_conv, sixth_conv, out_weight)
    xz_result = restore(jnp.transpose(volume, (1, 0, 2)), xz_tissue, weights)
    xz_result = jnp.transpose(xz_result, (1, 0, 2))
    yz_result = restore(jnp.transpose(volume, (2, 0, 1)), yz_tissue, weights)
    yz_result = jnp.transpose(yz_result, (1, 2, 0))
    averaged = 0.5 * (xz_result.astype(jnp.float32) + yz_result.astype(jnp.float32))
    return averaged.astype(jnp.bfloat16)
```

```python
import jax
import jax.numpy as jnp
from jax import lax
from jax.experimental import pallas as pl
from jax.experimental.pallas import tpu as pltpu
from jax.sharding import PartitionSpec as P

BF = jnp.bfloat16
F32 = jnp.float32
HALO = 8


def iota(shape, dim):
    return lax.broadcasted_iota(jnp.int32, shape, dim)


def dot(a, b):
    return jnp.dot(a, b, preferred_element_type=F32)


def spread(tap, cells):
    outs = tap.shape[1]
    shape = (outs, cells * outs)
    pick = (iota(shape, 0) == iota(shape, 1) % outs).astype(F32).astype(BF)
    return dot(tap, pick)


def stack_rows(tap, cells):
    return jnp.concatenate([tap] * cells, axis=0)


def prep_kernel(w1, w2, w3, w4, w5, w6, wo, t1, t2, t3, t4, t5, t6, th):
    def fine(src, dst, lo, hi, base):
        row, lane = iota((256, 256), 0) // 32, iota((256, 256), 1) // 32
        g = [spread(src[t, lo:hi, :], 8) for t in range(9)]
        edge = iota((32, 256), 1) // 32
        for s in range(3):
            tile = jnp.zeros((256, 256), F32)
            for r in range(3):
                tile = jnp.where(row == lane + (r - 1), stack_rows(g[3 * r + s], 8), tile)
            tile = tile.astype(BF)
            below = jnp.where(edge == 7, g[6 + s], 0.0).astype(BF)
            above = jnp.where(edge == 0, g[s], 0.0).astype(BF)
            for d in dst:
                d[0, 256 * s : 256 * s + 256, :] = tile
                d[1, 256 * s : 256 * s + 256, :] = tile
                d[0, base + 32 * s : base + 32 * s + 32, :] = below
                d[1, base + 32 * s : base + 32 * s + 32, :] = above

    fine(w2, [t2], 0, 32, 768)
    fine(w6, [t6], 0, 32, 768)
    fine(w5, [t5.at[0], t5.at[1]], 64, 96, 1280)

    row, lane = iota((16, 256), 0), iota((16, 256), 1) // 32
    for s in range(3):
        g = [spread(w1[3 * r + s, :, :], 8) for r in range(3)]
        for h in range(2):
            tile = jnp.zeros((16, 256), F32)
            for r in range(3):
                tile = jnp.where(row == lane + 8 * h + (r - 1), jnp.broadcast_to(g[r][0:1], (16, 256)), tile)
            t1[h, 16 * s : 16 * s + 16, :] = tile.astype(BF)

    row, lane = iota((256, 256), 0) // 32, iota((256, 256), 1) // 64
    g = [spread(w3[t, :, :], 4) for t in range(9)]
    for s in range(3):
        for h in range(2):
            tile = jnp.zeros((256, 256), F32)
            for r in range(3):
                tile = jnp.where(row == lane + 4 * h + (r - 1), stack_rows(g[3 * r + s], 8), tile)
            t3[h, 256 * s : 256 * s + 256, :] = tile.astype(BF)

    row, lane = iota((256, 256), 0) // 64, iota((256, 256), 1) // 64
    edge = iota((64, 256), 1) // 64
    g = [spread(w4[t, :, :], 4) for t in range(9)]
    for s in range(3):
        tile = jnp.zeros((256, 256), F32)
        for r in range(3):
            tile = jnp.where(row == lane + (r - 1), stack_rows(g[3 * r + s], 4), tile)
        tile = tile.astype(BF)
        for h in range(2):
            t4[h, 256 * s : 256 * s + 256, :] = tile
        t4[0, 768 + 64 * s : 832 + 64 * s, :] = jnp.where(edge == 3, g[6 + s], 0.0).astype(BF)
        t4[1, 768 + 64 * s : 832 + 64 * s, :] = jnp.where(edge == 0, g[s], 0.0).astype(BF)

    row, lane = iota((256, 256), 0) // 64, iota((256, 256), 1) // 32
    edge = iota((64, 256), 1) // 32
    g = [spread(w5[t, 0:64, :], 8) for t in range(9)]
    for q in range(2):
        groups = ((0,), (1, 2)) if q == 0 else ((0, 1), (2,))
        for i, taps in enumerate(groups):
            tile = jnp.zeros((256, 256), F32)
            for r in range(3):
                part = sum(g[3 * r + s] for s in taps)
                hit = row == ((lane + (r - 1) + 2) // 2 - 1)
                tile = tile + jnp.where(hit, stack_rows(part, 4), 0.0)
            tile = tile.astype(BF)
            for h in range(2):
                t5[q, h, 768 + 256 * i : 1024 + 256 * i, :] = tile
            below = sum(g[6 + s] for s in taps)
            above = sum(g[s] for s in taps)
            t5[q, 0, 1376 + 64 * i : 1440 + 64 * i, :] = jnp.where(edge == 7, below, 0.0).astype(BF)
            t5[q, 1, 1376 + 64 * i : 1440 + 64 * i, :] = jnp.where(edge == 0, above, 0.0).astype(BF)

    row, lane = iota((512, 128), 0), iota((512, 128), 1)
    pick = (iota((512, 32), 0) % 32 == iota((512, 32), 1)).astype(F32).astype(BF)
    column = dot(pick, wo[...])
    th[...] = jnp.where(row // 32 == lane, column, 0.0).astype(BF)


def prepare(w1, w2, w3, w4, w5, w6, wo):
    taps = [jnp.transpose(w, (1, 2, 0)) for w in (w1, w2, w3, w4, w5, w6)]
    head = jnp.broadcast_to(wo[:, None], (wo.shape[0], 128))
    shapes = [(2, 48, 256), (2, 864, 256), (2, 768, 256), (2, 960, 256), (2, 2, 1504, 256), (2, 864, 256), (512, 128)]
    return pl.pallas_call(
        prep_kernel,
        out_shape=[jax.ShapeDtypeStruct(s, BF) for s in shapes],
        cost_estimate=pl.CostEstimate(flops=400_000_000, bytes_accessed=5_000_000, transcendentals=0),
        name="prep",
    )(*taps, head)


def network(edges, n, wh, p, l1, a1, a2, pool, m1, m2, d1, weights, emit):
    t1, t2, t3, t4, t5, t6, th = weights
    pairs = wh + 8

    def rows(j, off, size):
        return pl.ds(pl.multiple_of((j + 4) * n + off, 16), size)

    def loop(count, cols, body):
        size = cols * n
        if count == cols:
            body(0, 0, size)
            return

        def step(i, carry):
            body(i * cols, i * size, size)
            return carry

        lax.fori_loop(0, count // cols, step, 0)

    def clear(ref, lead, first):
        for at in lead:
            for side, j, num in ((0, -first, first), (1, wh, first)):

                @pl.when(edges[side] > 0)
                def _(at=at, j=j, num=num):
                    ref[at + (rows(j, 0, num * n), slice(None))] = jnp.zeros((num * n, ref.shape[-1]), ref.dtype)

    both = [(0,), (1,)]
    four = [(q, h) for q in range(2) for h in range(2)]

    def near(q):
        return ((1, -1), (0, 0), (1, 0)) if q == 0 else ((0, 0), (1, 0), (0, 1))

    clear(p, both, 4)
    for q in range(2):
        j0 = -3 if q == 0 else -4
        size = (wh + 7) * n
        for s, (qs, dj) in enumerate(near(q)):
            l1[q, rows(j0, 0, size), 16 * s : 16 * s + 16] = p[qs, rows(j0 + dj, 0, size), :]

    def relu(v):
        return jnp.maximum(v, 0.0).astype(BF)

    c1 = {15: 5, 39: 13}[wh + 7]
    for q in range(2):
        j0 = -3 if q == 0 else -4

        def body(dj, off, size, q=q, j0=j0):
            r = rows(j0, off, size)
            x = l1[q, r, 0:48]
            for h in range(2):
                a1[q, h, r, :] = relu(dot(x, t1[h]))

        loop(wh + 7, c1, body)
    clear(a1, four, 4)

    def fine_inputs(src, q, h, j0, off, size):
        other = slice(0, 32) if h == 0 else slice(224, 256)
        own = [src[qs, h, rows(j0 + dj, off, size), :] for qs, dj in near(q)]
        edge = [src[qs, 1 - h, rows(j0 + dj, off, size), other] for qs, dj in near(q)]
        return own, edge

    c2 = (wh + 6) // 2
    for q, h in four:

        def body(dj, off, size, q=q, h=h):
            own, edge = fine_inputs(a1, q, h, -3, off, size)
            a2[q, h, rows(-3, off, size), :] = relu(dot(jnp.concatenate(own + edge, axis=1), t2[h]))

        loop(wh + 6, c2, body)
    clear(a2, four, 3)

    def pick_pool():
        shape = (1024, 256)
        row, lane = iota(shape, 0), iota(shape, 1)
        cell = 4 * (row // 512) + ((row // 32) % 8) // 2
        return jnp.where((cell == lane // 32) & (row % 32 == lane % 32), 0.25, 0.0).astype(BF)

    pm = pick_pool()

    def body(dj, off, size):
        r = rows(-3, off, size)
        x = jnp.concatenate([a2[0, 0, r, :], a2[1, 0, r, :], a2[0, 1, r, :], a2[1, 1, r, :]], axis=1)
        pool[r, :] = dot(x, pm).astype(BF)

    loop(wh + 6, c2, body)

    c3 = (wh + 4) // 2

    def body(dj, off, size):
        x = jnp.concatenate([pool[rows(-2 + k, off, size), :] for k in (-1, 0, 1)], axis=1)
        for h in range(2):
            m1[h, rows(-2, off, size), :] = relu(dot(x, t3[h]))

    loop(wh + 4, c3, body)
    clear(m1, both, 2)

    c4 = (wh + 2) // 2
    for h in range(2):

        def body(dj, off, size, h=h):
            other = slice(0, 64) if h == 0 else slice(192, 256)
            own = [m1[h, rows(-1 + k, off, size), :] for k in (-1, 0, 1)]
            edge = [m1[1 - h, rows(-1 + k, off, size), other] for k in (-1, 0, 1)]
            m2[h, rows(-1, off, size), :] = relu(dot(jnp.concatenate(own + edge, axis=1), t4[h]))

        loop(wh + 2, c4, body)
    clear(m2, both, 1)

    c5 = {9: 3, 33: 11}[wh + 1]
    for q, h in four:
        j0 = 0 if q == 0 else -1

        def body(dj, off, size, q=q, h=h, j0=j0):
            own, edge = fine_inputs(a2, q, h, j0, off, size)
            other = slice(0, 64) if h == 0 else slice(192, 256)
            cells = (-1, 0) if q == 0 else (0, 1)
            own += [m2[h, rows(j0 + k, off, size), :] for k in cells]
            edge += [m2[1 - h, rows(j0 + k, off, size), other] for k in cells]
            d1[q, h, rows(j0, off, size), :] = relu(dot(jnp.concatenate(own + edge, axis=1), t5[q, h]))

        loop(wh + 1, c5, body)
    clear(d1, four, 1)

    c6 = wh // 2
    for q in range(2):

        def body(dj, off, size, q=q):
            parts = []
            for h in range(2):
                own, edge = fine_inputs(d1, q, h, 0, off, size)
                parts.append(relu(dot(jnp.concatenate(own + edge, axis=1), t6[h])))
            emit(q, dj, c6, dot(jnp.concatenate(parts, axis=1), th[...]))

        loop(wh, c6, body)


def unet_scratch(n, wh):
    m = (wh + 8) * n
    return [
        pltpu.VMEM((2, m, 16), BF),
        pltpu.VMEM((2, m, 128), BF),
        pltpu.VMEM((2, 2, m, 256), BF),
        pltpu.VMEM((2, 2, m, 256), BF),
        pltpu.VMEM((m, 256), BF),
        pltpu.VMEM((2, m, 256), BF),
        pltpu.VMEM((2, m, 256), BF),
        pltpu.VMEM((2, 2, m, 256), BF),
    ]


def xz_kernel(edges, v, *refs):
    weights, (out, vf, pf, hx), scratch = refs[:7], refs[7:11], refs[11:]
    n, wh = 16, 32
    for z in range(16):
        vf[16 * z : 16 * z + 16, :] = v[z].astype(F32)
    for y in range(16):
        turned = jnp.transpose(vf[pl.ds(y, 16, stride=16), :])
        pf[pl.ds(y, 80, stride=16), 0:16] = turned[0:80, :]
    p = scratch[0]
    for x in range(80):
        p[x % 2, 16 * (x // 2) : 16 * (x // 2) + 16, :] = pf[16 * x : 16 * x + 16, 0:16].astype(BF)

    def emit(q, j0, cols, head):
        for k in range(cols):
            at = pl.multiple_of((2 * (j0 + k) + q) * n, 16)
            hx[pl.ds(at, n), :] = head[k * n : k * n + n, :]

    network(edges, n, wh, *scratch, weights, emit)
    for y in range(16):
        out[y] = jnp.transpose(hx[pl.ds(y, 64, stride=16), :])[0:16, :]


def yz_kernel(edges, xflags, v, before, after, yflags, xz, *refs):
    weights, (out, vf, hf, hy, rf), scratch = refs[:7], refs[7:12], refs[12:]
    n, wh = 64, 8
    p = scratch[0]
    for z in range(16):
        vf[16 * z : 16 * z + 16, :] = v[z].astype(F32)
        hf[16 * z : 16 * z + 8, :] = before[z, 8:16, :].astype(F32)
        hf[16 * z + 8 : 16 * z + 16, :] = after[z, 0:8, :].astype(F32)
    for k in range(32):
        if k < 8:
            plane = hf[pl.ds(k, 16, stride=16), :]
        elif k < 24:
            plane = vf[pl.ds(k - 8, 16, stride=16), :]
        else:
            plane = hf[pl.ds(k - 16, 16, stride=16), :]
        turned = jnp.transpose(plane)
        p[k % 2, n * (k // 2) : n * (k // 2) + n, :] = turned[HALO : HALO + n, :].astype(BF)

    def emit(q, j0, cols, head):
        for k in range(cols):
            at = pl.multiple_of((2 * (j0 + k) + q) * n, 16)
            hy[pl.ds(at, n), :] = head[k * n : k * n + n, :]

    network(edges, n, wh, *scratch, weights, emit)

    yes = yflags[...] > 0
    for y in range(16):
        plane = pltpu.roll(vf[pl.ds(y, 16, stride=16), :], 128 - HALO, 1)[:, 0:64]
        yz = jnp.transpose(hy[64 * y : 64 * y + 64, :])[0:16, :]
        yz = jnp.where(yes, plane + yz, plane).astype(BF).astype(F32)
        xz_new = (plane + xz[y]).astype(BF).astype(F32)
        xz_new = jnp.where(xflags[y] > 0, xz_new, plane)
        rf[pl.ds(y, 16, stride=16), 0:64] = 0.5 * (xz_new + yz)
    for z in range(16):
        block = rf[16 * z : 16 * z + 16, 0:64].astype(BF)
        out[2 * (z // 2), z % 2] = block
        out[2 * (z // 2) + 1, z % 2] = block


def pack_kernel(side, v, out):
    for c, shift in ((0, HALO), (1, 1024 + HALO - 64)):

        @pl.when(side[0] == c)
        def _(shift=shift):
            for z in range(2):
                rolled = pltpu.roll(v[z].astype(F32), shift, 1).astype(BF)
                for s in range(8):
                    out[s, z] = rolled[:, 128 * s : 128 * s + 128]


SMEM = pl.BlockSpec(memory_space=pltpu.SMEM)
VMEM = pl.BlockSpec(memory_space=pltpu.VMEM)


def per_device(volume, xz_tissue, yz_tissue, *weights):
    slab, tile, ch = lax.axis_index("slab"), lax.axis_index("tile"), lax.axis_index("ch")
    packed = pl.pallas_call(
        pack_kernel,
        out_shape=jax.ShapeDtypeStruct((8, 2, 16, 128), BF),
        in_specs=[SMEM, VMEM],
        out_specs=VMEM,
        name="pack",
    )(ch[None].astype(jnp.int32), volume)
    moved = lax.all_to_all(packed, "slab", split_axis=0, concat_axis=0, tiled=True)
    v = moved.reshape(16, 16, 128)
    tables = prepare(*weights)

    flags = yz_tissue
    for bit in (1, 2, 4, 8):
        other = lax.ppermute(flags, "tile", [(i, i ^ bit) for i in range(16)])
        high = (tile & bit) > 0
        flags = jnp.where(high, jnp.concatenate([other, flags]), jnp.concatenate([flags, other]))
    yflags = lax.dynamic_slice_in_dim(flags, 64 * ch, 64, 0)[None, :]

    before = lax.ppermute(v, "tile", [(i, i + 1) for i in range(15)])
    after = lax.ppermute(v, "tile", [(i + 1, i) for i in range(15)])

    window = 2 * slab + ch
    xz_edges = jnp.stack([window == 0, window == 15]).astype(jnp.int32)
    yz_edges = jnp.stack([tile == 0, tile == 15]).astype(jnp.int32)

    xz = pl.pallas_call(
        xz_kernel,
        out_shape=jax.ShapeDtypeStruct((16, 16, 64), F32),
        in_specs=[SMEM] + [VMEM] * 8,
        out_specs=VMEM,
        scratch_shapes=[pltpu.VMEM((256, 128), F32), pltpu.VMEM((1280, 128), F32), pltpu.VMEM((1024, 128), F32)]
        + unet_scratch(16, 32),
        cost_estimate=pl.CostEstimate(flops=6_000_000_000, bytes_accessed=6_000_000, transcendentals=0),
        name="xz",
    )(xz_edges, v, *tables)

    block = pl.pallas_call(
        yz_kernel,
        out_shape=jax.ShapeDtypeStruct((16, 2, 16, 64), BF),
        in_specs=[SMEM, SMEM] + [VMEM] * 12,
        out_specs=VMEM,
        scratch_shapes=[
            pltpu.VMEM((256, 128), F32),
            pltpu.VMEM((256, 128), F32),
            pltpu.VMEM((1024, 128), F32),
            pltpu.VMEM((256, 128), F32),
        ]
        + unet_scratch(64, 8),
        cost_estimate=pl.CostEstimate(flops=6_000_000_000, bytes_accessed=6_000_000, transcendentals=0),
        name="yz",
    )(yz_edges, xz_tissue, v, before, after, yflags, xz, *tables)

    back = lax.all_to_all(block, ("slab", "ch"), split_axis=0, concat_axis=0, tiled=True)
    return jnp.transpose(back, (1, 2, 0, 3)).reshape(2, 16, 1024)


def solution(mesh):
    return jax.shard_map(
        per_device,
        mesh=mesh,
        in_specs=(P("slab", "tile", None), P("tile"), P(("slab", "tile"))) + (P(),) * 7,
        out_specs=P("slab", "tile", None),
        check_vma=False,
    )
```

```python
import jax
import jax.numpy as jnp
from jax import lax
from jax.experimental import pallas as pl
from jax.experimental.pallas import tpu as pltpu
from jax.sharding import PartitionSpec as P


BF = jnp.bfloat16
F32 = jnp.float32
SMEM = pl.BlockSpec(memory_space=pltpu.SMEM)
VMEM = pl.BlockSpec(memory_space=pltpu.VMEM)
HALO = 8


def iota(shape, dim):
    return lax.broadcasted_iota(jnp.int32, shape, dim)


def dot(a, b):
    return jnp.dot(a, b, preferred_element_type=F32)


def spread(tap, cells, out_first):
    outs = tap.shape[0 if out_first else 1]
    shape = (outs, cells * outs)
    pick = (iota(shape, 0) == iota(shape, 1) % outs).astype(F32).astype(BF)
    dims = (((0 if out_first else 1,), (0,)), ((), ()))
    return lax.dot_general(tap, pick, dims, preferred_element_type=F32)


def stack_rows(tap, cells):
    return jnp.concatenate([tap] * cells, axis=0)


def build_tables(held, t1, t2, t3, t4, t5, t6, th):
    def part(first, last):
        return lambda t, lo, hi: held[t, first:last, lo:hi]

    w2, w3, w4, w5, w6 = part(0, 32), part(32, 64), part(64, 128), part(128, 160), part(160, 192)

    def fine(src, dst, lo, hi, base):
        row, lane = iota((256, 256), 0) // 32, iota((256, 256), 1) // 32
        g = [spread(src(t, lo, hi), 8, True) for t in range(9)]
        edge = iota((32, 256), 1) // 32
        for s in range(3):
            tile = jnp.zeros((256, 256), F32)
            for r in range(3):
                tile = jnp.where(row == lane + (r - 1), stack_rows(g[3 * r + s], 8), tile)
            tile = tile.astype(BF)
            below = jnp.where(edge == 7, g[6 + s], 0.0).astype(BF)
            above = jnp.where(edge == 0, g[s], 0.0).astype(BF)
            for d in dst:
                d[0, 256 * s : 256 * s + 256, :] = tile
                d[1, 256 * s : 256 * s + 256, :] = tile
                d[0, base + 32 * s : base + 32 * s + 32, :] = below
                d[1, base + 32 * s : base + 32 * s + 32, :] = above

    fine(w2, [t2], 0, 32, 768)
    fine(w6, [t6], 0, 32, 768)
    fine(w5, [t5.at[0], t5.at[1]], 64, 96, 1280)

    row, lane = iota((16, 256), 0), iota((16, 256), 1) // 32
    first = spread(held[9, 0:16, 0:32], 8, False)
    for s in range(3):
        g = [first[3 * r + s : 3 * r + s + 1, :] for r in range(3)]
        for h in range(2):
            tile = jnp.zeros((16, 256), F32)
            for r in range(3):
                tile = jnp.where(row == lane + 8 * h + (r - 1), jnp.broadcast_to(g[r], (16, 256)), tile)
            t1[h, 16 * s : 16 * s + 16, :] = tile.astype(BF)

    row, lane = iota((256, 256), 0) // 32, iota((256, 256), 1) // 64
    g = [spread(w3(t, 0, 64), 4, False) for t in range(9)]
    for s in range(3):
        for h in range(2):
            tile = jnp.zeros((256, 256), F32)
            for r in range(3):
                tile = jnp.where(row == lane + 4 * h + (r - 1), stack_rows(g[3 * r + s], 8), tile)
            t3[h, 256 * s : 256 * s + 256, :] = tile.astype(BF)

    row, lane = iota((256, 256), 0) // 64, iota((256, 256), 1) // 64
    edge = iota((64, 256), 1) // 64
    g = [spread(w4(t, 0, 64), 4, True) for t in range(9)]
    for s in range(3):
        tile = jnp.zeros((256, 256), F32)
        for r in range(3):
            tile = jnp.where(row == lane + (r - 1), stack_rows(g[3 * r + s], 4), tile)
        tile = tile.astype(BF)
        for h in range(2):
            t4[h, 256 * s : 256 * s + 256, :] = tile
        t4[0, 768 + 64 * s : 832 + 64 * s, :] = jnp.where(edge == 3, g[6 + s], 0.0).astype(BF)
        t4[1, 768 + 64 * s : 832 + 64 * s, :] = jnp.where(edge == 0, g[s], 0.0).astype(BF)

    row, lane = iota((256, 256), 0) // 64, iota((256, 256), 1) // 32
    edge = iota((64, 256), 1) // 32
    g = [spread(w5(t, 0, 64), 8, True) for t in range(9)]
    for q in range(2):
        groups = ((0,), (1, 2)) if q == 0 else ((0, 1), (2,))
        for i, taps in enumerate(groups):
            tile = jnp.zeros((256, 256), F32)
            for r in range(3):
                part = sum(g[3 * r + s] for s in taps)
                hit = row == ((lane + (r - 1) + 2) // 2 - 1)
                tile = tile + jnp.where(hit, stack_rows(part, 4), 0.0)
            tile = tile.astype(BF)
            for h in range(2):
                t5[q, h, 768 + 256 * i : 1024 + 256 * i, :] = tile
            below = sum(g[6 + s] for s in taps)
            above = sum(g[s] for s in taps)
            t5[q, 0, 1376 + 64 * i : 1440 + 64 * i, :] = jnp.where(edge == 7, below, 0.0).astype(BF)
            t5[q, 1, 1376 + 64 * i : 1440 + 64 * i, :] = jnp.where(edge == 0, above, 0.0).astype(BF)

    row, lane = iota((512, 128), 0), iota((512, 128), 1)
    pick = (iota((512, 32), 0) % 32 == iota((512, 32), 1)).astype(F32)
    column = jnp.sum(pick * held[9, 16:32, 0:32].astype(F32)[0:1], axis=1, keepdims=True)
    th[...] = jnp.where(row // 32 == lane, column, 0.0).astype(BF)


def stage_kernel(w1, w2, w3, w4, w5, w6, wo, out):
    for t in range(9):
        out[t, 0:32, 0:32] = w2[t]
        out[t, 32:64, 0:64] = w3[t]
        out[t, 64:128, 0:64] = w4[t]
        out[t, 128:160, 0:96] = w5[t]
        out[t, 160:192, 0:32] = w6[t]
    out[9, 0:32, :] = jnp.zeros((32, 128), BF)
    out[9, 0:9, 0:32] = w1[...]
    out[9, 16:17, 0:32] = wo[...]


def stage(raw):
    return pl.pallas_call(
        stage_kernel,
        out_shape=jax.ShapeDtypeStruct((10, 192, 128), BF),
        in_specs=[VMEM] * 7,
        out_specs=VMEM,
        name="stage",
    )(*raw)


def prepare(w1, w2, w3, w4, w5, w6, wo):
    taps = [jnp.transpose(w1[:, :, 0])] + [jnp.transpose(w, (1, 0, 2)) for w in (w2, w3, w4, w5, w6)]
    taps[2] = jnp.transpose(w3, (1, 2, 0))
    return taps + [wo[None, :]]


TABLES = [(2, 48, 256), (2, 864, 256), (2, 768, 256), (2, 960, 256), (2, 2, 1504, 256), (2, 864, 256), (512, 128)]


def network(edges, n, wh, p, l1, a1, a2, pool, m1, m2, d1, weights, emit):
    t1, t2, t3, t4, t5, t6, th = weights

    def rows(j, off, size):
        return pl.ds(pl.multiple_of((j + 4) * n + off, 16), size)

    def loop(count, cols, body):
        size = cols * n
        if count == cols:
            body(0, 0, size)
            return

        def step(i, carry):
            body(i * cols, i * size, size)
            return carry

        lax.fori_loop(0, count // cols, step, 0)

    def clear(ref, lead, first):
        for at in lead:
            for side, j, num in ((0, -first, first), (1, wh, first)):

                @pl.when(edges[side] > 0)
                def _(at=at, j=j, num=num):
                    ref[at + (rows(j, 0, num * n), slice(None))] = jnp.zeros((num * n, ref.shape[-1]), ref.dtype)

    both = [(0,), (1,)]
    four = [(q, h) for q in range(2) for h in range(2)]

    def near(q):
        return ((1, -1), (0, 0), (1, 0)) if q == 0 else ((0, 0), (1, 0), (0, 1))

    clear(p, both, 4)
    for q in range(2):
        j0 = -3 if q == 0 else -4
        size = (wh + 7) * n
        for s, (qs, dj) in enumerate(near(q)):
            l1[q, rows(j0, 0, size), 16 * s : 16 * s + 16] = p[qs, rows(j0 + dj, 0, size), :]

    def relu(v):
        return jnp.maximum(v, 0.0).astype(BF)

    c1 = {15: 5, 39: 13}[wh + 7]
    for q in range(2):
        j0 = -3 if q == 0 else -4

        def body(dj, off, size, q=q, j0=j0):
            r = rows(j0, off, size)
            x = l1[q, r, 0:48]
            for h in range(2):
                a1[q, h, r, :] = relu(dot(x, t1[h]))

        loop(wh + 7, c1, body)
    clear(a1, four, 4)

    def fine_inputs(src, q, h, j0, off, size):
        other = slice(0, 32) if h == 0 else slice(224, 256)
        own = [src[qs, h, rows(j0 + dj, off, size), :] for qs, dj in near(q)]
        edge = [src[qs, 1 - h, rows(j0 + dj, off, size), other] for qs, dj in near(q)]
        return own, edge

    c2 = (wh + 6) // 2
    for q, h in four:

        def body(dj, off, size, q=q, h=h):
            own, edge = fine_inputs(a1, q, h, -3, off, size)
            a2[q, h, rows(-3, off, size), :] = relu(dot(jnp.concatenate(own + edge, axis=1), t2[h]))

        loop(wh + 6, c2, body)
    clear(a2, four, 3)

    def pick_pool():
        shape = (1024, 256)
        row, lane = iota(shape, 0), iota(shape, 1)
        cell = 4 * (row // 512) + ((row // 32) % 8) // 2
        return jnp.where((cell == lane // 32) & (row % 32 == lane % 32), 0.25, 0.0).astype(BF)

    pm = pick_pool()

    def body(dj, off, size):
        r = rows(-3, off, size)
        x = jnp.concatenate([a2[0, 0, r, :], a2[1, 0, r, :], a2[0, 1, r, :], a2[1, 1, r, :]], axis=1)
        pool[r, :] = dot(x, pm).astype(BF)

    loop(wh + 6, c2, body)

    c3 = (wh + 4) // 2

    def body(dj, off, size):
        x = jnp.concatenate([pool[rows(-2 + k, off, size), :] for k in (-1, 0, 1)], axis=1)
        for h in range(2):
            m1[h, rows(-2, off, size), :] = relu(dot(x, t3[h]))

    loop(wh + 4, c3, body)
    clear(m1, both, 2)

    c4 = (wh + 2) // 2
    for h in range(2):

        def body(dj, off, size, h=h):
            other = slice(0, 64) if h == 0 else slice(192, 256)
            own = [m1[h, rows(-1 + k, off, size), :] for k in (-1, 0, 1)]
            edge = [m1[1 - h, rows(-1 + k, off, size), other] for k in (-1, 0, 1)]
            m2[h, rows(-1, off, size), :] = relu(dot(jnp.concatenate(own + edge, axis=1), t4[h]))

        loop(wh + 2, c4, body)
    clear(m2, both, 1)

    c5 = {9: 3, 33: 11}[wh + 1]
    for q, h in four:
        j0 = 0 if q == 0 else -1

        def body(dj, off, size, q=q, h=h, j0=j0):
            own, edge = fine_inputs(a2, q, h, j0, off, size)
            other = slice(0, 64) if h == 0 else slice(192, 256)
            cells = (-1, 0) if q == 0 else (0, 1)
            own += [m2[h, rows(j0 + k, off, size), :] for k in cells]
            edge += [m2[1 - h, rows(j0 + k, off, size), other] for k in cells]
            d1[q, h, rows(j0, off, size), :] = relu(dot(jnp.concatenate(own + edge, axis=1), t5[q, h]))

        loop(wh + 1, c5, body)
    clear(d1, four, 1)

    c6 = wh // 2
    for q in range(2):

        def body(dj, off, size, q=q):
            parts = []
            for h in range(2):
                own, edge = fine_inputs(d1, q, h, 0, off, size)
                parts.append(relu(dot(jnp.concatenate(own + edge, axis=1), t6[h])))
            emit(q, dj, c6, dot(jnp.concatenate(parts, axis=1), th[...]))

        loop(wh, c6, body)


def unet_scratch(n, wh):
    m = (wh + 8) * n
    return [
        pltpu.VMEM((2, m, 16), BF),
        pltpu.VMEM((2, m, 128), BF),
        pltpu.VMEM((2, 2, m, 256), BF),
        pltpu.VMEM((2, 2, m, 256), BF),
        pltpu.VMEM((m, 256), BF),
        pltpu.VMEM((2, m, 256), BF),
        pltpu.VMEM((2, m, 256), BF),
        pltpu.VMEM((2, 2, m, 256), BF),
    ]


def xz_kernel(edges, v, *refs):
    held, out, weights, (vf, pf, hx), scratch = refs[0], refs[1], refs[2:9], refs[9:12], refs[12:]
    n, wh = 16, 32
    for z in range(16):
        vf[16 * z : 16 * z + 16, :] = v[z].astype(F32)
    for y in range(16):
        turned = jnp.transpose(vf[pl.ds(y, 16, stride=16), :])
        pf[pl.ds(y, 80, stride=16), 0:16] = turned[0:80, :]
    p = scratch[0]
    for x in range(80):
        p[x % 2, 16 * (x // 2) : 16 * (x // 2) + 16, :] = pf[16 * x : 16 * x + 16, 0:16].astype(BF)

    build_tables(held, *weights)

    def emit(q, j0, cols, head):
        for k in range(cols):
            at = pl.multiple_of((2 * (j0 + k) + q) * n, 16)
            hx[pl.ds(at, n), :] = head[k * n : k * n + n, :]

    network(edges, n, wh, *scratch, weights, emit)
    for y in range(16):
        out[y] = jnp.transpose(hx[pl.ds(y, 64, stride=16), :])[0:16, :]


def yz_kernel(edges, xflags, v, before, after, yflags, xz, *refs):
    weights, (out, vf, hf, hy, rf), scratch = refs[:7], refs[7:12], refs[12:]
    n, wh = 64, 8
    p = scratch[0]
    for z in range(16):
        vf[16 * z : 16 * z + 16, :] = v[z].astype(F32)
        hf[16 * z : 16 * z + 8, :] = before[z, 8:16, :].astype(F32)
        hf[16 * z + 8 : 16 * z + 16, :] = after[z, 0:8, :].astype(F32)
    for k in range(32):
        if k < 8:
            plane = hf[pl.ds(k, 16, stride=16), :]
        elif k < 24:
            plane = vf[pl.ds(k - 8, 16, stride=16), :]
        else:
            plane = hf[pl.ds(k - 16, 16, stride=16), :]
        turned = jnp.transpose(plane)
        p[k % 2, n * (k // 2) : n * (k // 2) + n, :] = turned[HALO : HALO + n, :].astype(BF)

    def emit(q, j0, cols, head):
        for k in range(cols):
            at = pl.multiple_of((2 * (j0 + k) + q) * n, 16)
            hy[pl.ds(at, n), :] = head[k * n : k * n + n, :]

    network(edges, n, wh, *scratch, weights, emit)

    yes = yflags[...] > 0
    for y in range(16):
        plane = pltpu.roll(vf[pl.ds(y, 16, stride=16), :], 128 - HALO, 1)[:, 0:64]
        yz = jnp.transpose(hy[64 * y : 64 * y + 64, :])[0:16, :]
        yz = jnp.where(yes, plane + yz, plane).astype(BF).astype(F32)
        xz_new = (plane + xz[y]).astype(BF).astype(F32)
        xz_new = jnp.where(xflags[y] > 0, xz_new, plane)
        rf[pl.ds(y, 16, stride=16), 0:64] = 0.5 * (xz_new + yz)
    for z in range(16):
        block = rf[16 * z : 16 * z + 16, 0:64].astype(BF)
        out[2 * (z // 2), z % 2] = block
        out[2 * (z // 2) + 1, z % 2] = block


def pack_kernel(side, v, out):
    for c, shift in ((0, HALO), (1, 1024 + HALO - 64)):

        @pl.when(side[0] == c)
        def _(shift=shift):
            for z in range(2):
                rolled = pltpu.roll(v[z].astype(F32), shift, 1).astype(BF)
                for s in range(8):
                    out[s, z] = rolled[:, 128 * s : 128 * s + 128]


def compute(xz_edges, yz_edges, xz_tissue, yflags, v, before, after, raw):
    xz, *tables = pl.pallas_call(
        xz_kernel,
        out_shape=[jax.ShapeDtypeStruct((16, 16, 64), F32)] + [jax.ShapeDtypeStruct(s, BF) for s in TABLES],
        in_specs=[SMEM, VMEM, VMEM],
        out_specs=[VMEM] * 8,
        scratch_shapes=[pltpu.VMEM((256, 128), F32), pltpu.VMEM((1280, 128), F32), pltpu.VMEM((1024, 128), F32)]
        + unet_scratch(16, 32),
        compiler_params=pltpu.CompilerParams(vmem_limit_bytes=24 << 20),
        cost_estimate=pl.CostEstimate(flops=6_000_000_000, bytes_accessed=6_000_000, transcendentals=0),
        name="xz",
    )(xz_edges, v, raw)
    return pl.pallas_call(
        yz_kernel,
        out_shape=jax.ShapeDtypeStruct((16, 2, 16, 64), BF),
        in_specs=[SMEM, SMEM] + [VMEM] * 12,
        out_specs=VMEM,
        scratch_shapes=[
            pltpu.VMEM((256, 128), F32),
            pltpu.VMEM((256, 128), F32),
            pltpu.VMEM((1024, 128), F32),
            pltpu.VMEM((256, 128), F32),
        ]
        + unet_scratch(64, 8),
        compiler_params=pltpu.CompilerParams(vmem_limit_bytes=24 << 20),
        cost_estimate=pl.CostEstimate(flops=6_000_000_000, bytes_accessed=6_000_000, transcendentals=0),
        name="yz",
    )(yz_edges, xz_tissue, v, before, after, yflags, xz, *tables)


def per_device(volume, xz_tissue, yz_tissue, *weights):
    slab, tile, ch = lax.axis_index("slab"), lax.axis_index("tile"), lax.axis_index("ch")
    packed = pl.pallas_call(
        pack_kernel,
        out_shape=jax.ShapeDtypeStruct((8, 2, 16, 128), BF),
        in_specs=[SMEM, VMEM],
        out_specs=VMEM,
        name="pack",
    )(ch[None].astype(jnp.int32), volume)
    moved = lax.all_to_all(packed, "slab", split_axis=0, concat_axis=0, tiled=True)
    v = moved.reshape(16, 16, 128)
    raw = stage(prepare(*weights))

    flags = yz_tissue
    for bit in (1, 2, 4, 8):
        other = lax.ppermute(flags, "tile", [(i, i ^ bit) for i in range(16)])
        high = (tile & bit) > 0
        flags = jnp.where(high, jnp.concatenate([other, flags]), jnp.concatenate([flags, other]))
    yflags = lax.dynamic_slice_in_dim(flags, 64 * ch, 64, 0)[None, :]

    before = lax.ppermute(v, "tile", [(i, i + 1) for i in range(15)])
    after = lax.ppermute(v, "tile", [(i + 1, i) for i in range(15)])

    window = 2 * slab + ch
    xz_edges = jnp.stack([window == 0, window == 15]).astype(jnp.int32)
    yz_edges = jnp.stack([tile == 0, tile == 15]).astype(jnp.int32)

    block = compute(xz_edges, yz_edges, xz_tissue, yflags, v, before, after, raw)
    back = lax.all_to_all(block, ("slab", "ch"), split_axis=0, concat_axis=0, tiled=True)
    return jnp.transpose(back, (1, 2, 0, 3)).reshape(2, 16, 1024)


def solution(mesh):
    return jax.shard_map(
        per_device,
        mesh=mesh,
        in_specs=(P("slab", "tile", None), P("tile"), P(("slab", "tile"))) + (P(),) * 7,
        out_specs=P("slab", "tile", None),
        check_vma=False,
    )
```

```python
import jax
import jax.numpy as jnp
from jax import lax
from jax.experimental import pallas as pl
from jax.experimental.pallas import tpu as pltpu
from jax.sharding import PartitionSpec as P

BF = jnp.bfloat16
F32 = jnp.float32
SMEM = pl.BlockSpec(memory_space=pltpu.SMEM)
VMEM = pl.BlockSpec(memory_space=pltpu.VMEM)
HALO = 8


def iota(shape, dim):
    return lax.broadcasted_iota(jnp.int32, shape, dim)


def dot(a, b):
    return jnp.dot(a, b, preferred_element_type=F32)


def spread(tap, cells, out_first):
    outs = tap.shape[0 if out_first else 1]
    shape = (outs, cells * outs)
    pick = (iota(shape, 0) == iota(shape, 1) % outs).astype(F32).astype(BF)
    dims = (((0 if out_first else 1,), (0,)), ((), ()))
    return lax.dot_general(tap, pick, dims, preferred_element_type=F32)


def stack_rows(tap, cells):
    return jnp.concatenate([tap] * cells, axis=0)


def taps_of(held, first, last):
    return lambda t, lo, hi: held[t, first:last, lo:hi]


def fine(src, lo, hi, base, own, edges, merged):
    row, lane = iota((256, 256), 0) // 32, iota((256, 256), 1) // 32
    g = [spread(src(t, lo, hi), 8, True) for t in range(9)]
    edge = iota((32, 256), 1) // 32
    for s in range(3):
        tile = jnp.zeros((256, 256), F32)
        for r in range(3):
            tile = jnp.where(row == lane + (r - 1), stack_rows(g[3 * r + s], 8), tile)
        tile = tile.astype(BF)
        for d in own:
            d[256 * s : 256 * s + 256, :] = tile
        for h, near, taps in ((0, 7, g[6 + s]), (1, 0, g[s])):
            for d in edges:
                d[h, base + 32 * s : base + 32 * s + 32, :] = jnp.where(edge == near, taps, 0.0).astype(BF)
    for d in merged:
        for h in range(2):
            for k in range(4):
                tile = jnp.zeros((32, 256), F32)
                for q in range(2):
                    s = k - q
                    if 0 <= s < 3:
                        near = (7, 3)[q] if h == 0 else (0, 4)[q]
                        tile = jnp.where(edge == near, g[6 + s] if h == 0 else g[s], tile)
                d[128 * h + 32 * k : 128 * h + 32 * k + 32, :] = tile.astype(BF)


def build_tables(held, t1, t2, t3, t4, t6):
    w2, w3, w4, w6 = taps_of(held, 0, 32), taps_of(held, 32, 64), taps_of(held, 64, 128), taps_of(held, 160, 192)

    fine(w2, 0, 32, 0, [t2.at[0:768]], [], [t2.at[768:1024]])
    fine(w6, 0, 32, 0, [t6.at[0:768]], [], [t6.at[768:1024]])

    row, lane = iota((16, 256), 0), iota((16, 256), 1) // 32
    first = spread(held[9, 0:16, 0:32], 8, False)
    for s in range(3):
        g = [first[3 * r + s : 3 * r + s + 1, :] for r in range(3)]
        for h in range(2):
            tile = jnp.zeros((16, 256), F32)
            for r in range(3):
                tile = jnp.where(row == lane + 8 * h + (r - 1), jnp.broadcast_to(g[r], (16, 256)), tile)
            t1[h, 16 * s : 16 * s + 16, :] = tile.astype(BF)

    row, lane = iota((256, 256), 0) // 32, iota((256, 256), 1) // 64
    row = row // 2 + 4 * (row % 2)
    g = [spread(w3(t, 0, 64), 4, False) for t in range(9)]
    for s in range(3):
        for h in range(2):
            tile = jnp.zeros((256, 256), F32)
            for r in range(3):
                tile = jnp.where(row == lane + 4 * h + (r - 1), stack_rows(g[3 * r + s], 8), tile)
            t3[256 * s : 256 * s + 256, 256 * h : 256 * h + 256] = tile.astype(BF)

    row, lane = iota((256, 256), 0) // 64, iota((256, 256), 1) // 64
    edge = iota((64, 256), 1) // 64
    g = [spread(w4(t, 0, 64), 4, True) for t in range(9)]
    for s in range(3):
        tile = jnp.zeros((256, 256), F32)
        for r in range(3):
            tile = jnp.where(row == lane + (r - 1), stack_rows(g[3 * r + s], 4), tile)
        tile = tile.astype(BF)
        for h in range(2):
            t4[h, 256 * s : 256 * s + 256, :] = tile
        t4[0, 768 + 64 * s : 832 + 64 * s, :] = jnp.where(edge == 3, g[6 + s], 0.0).astype(BF)
        t4[1, 768 + 64 * s : 832 + 64 * s, :] = jnp.where(edge == 0, g[s], 0.0).astype(BF)


def build_join(held, t5, th):
    w5 = taps_of(held, 128, 160)
    fine(w5, 64, 96, 1280, [t5.at[q, h] for q in range(2) for h in range(2)], [t5.at[0], t5.at[1]], [])

    row, lane = iota((256, 256), 0) // 64, iota((256, 256), 1) // 32
    edge = iota((64, 256), 1) // 32
    g = [spread(w5(t, 0, 64), 8, True) for t in range(9)]
    for q in range(2):
        groups = ((0,), (1, 2)) if q == 0 else ((0, 1), (2,))
        for i, taps in enumerate(groups):
            tile = jnp.zeros((256, 256), F32)
            for r in range(3):
                part = sum(g[3 * r + s] for s in taps)
                hit = row == ((lane + (r - 1) + 2) // 2 - 1)
                tile = tile + jnp.where(hit, stack_rows(part, 4), 0.0)
            tile = tile.astype(BF)
            for h in range(2):
                t5[q, h, 768 + 256 * i : 1024 + 256 * i, :] = tile
            below = sum(g[6 + s] for s in taps)
            above = sum(g[s] for s in taps)
            t5[q, 0, 1376 + 64 * i : 1440 + 64 * i, :] = jnp.where(edge == 7, below, 0.0).astype(BF)
            t5[q, 1, 1376 + 64 * i : 1440 + 64 * i, :] = jnp.where(edge == 0, above, 0.0).astype(BF)

    row, lane = iota((512, 128), 0), iota((512, 128), 1)
    pick = (iota((512, 32), 0) % 32 == iota((512, 32), 1)).astype(F32)
    column = jnp.sum(pick * held[9, 16:32, 0:32].astype(F32)[0:1], axis=1, keepdims=True)
    th[...] = jnp.where(row // 32 == lane, column, 0.0).astype(BF)


def stage_kernel(w1, w2, w3, w4, w5, w6, wo, out):
    for t in range(9):
        out[t, 0:32, 0:32] = w2[t]
        out[t, 32:64, 0:64] = w3[t]
        out[t, 64:128, 0:64] = w4[t]
        out[t, 128:160, 0:96] = w5[t]
        out[t, 160:192, 0:32] = w6[t]
    out[9, 0:32, :] = jnp.zeros((32, 128), BF)
    out[9, 0:9, 0:32] = w1[...]
    out[9, 16:17, 0:32] = wo[...]


def stage(raw):
    return pl.pallas_call(
        stage_kernel,
        out_shape=jax.ShapeDtypeStruct((10, 192, 128), BF),
        in_specs=[VMEM] * 7,
        out_specs=VMEM,
        name="stage",
    )(*raw)


def prepare(w1, w2, w3, w4, w5, w6, wo):
    taps = [jnp.transpose(w1[:, :, 0])] + [jnp.transpose(w, (1, 0, 2)) for w in (w2, w3, w4, w5, w6)]
    taps[2] = jnp.transpose(w3, (1, 2, 0))
    return taps + [wo[None, :]]


TABLES = [(2, 48, 256), (1024, 256), (768, 512), (2, 960, 256), (1024, 256)]
JOIN = [(2, 2, 1504, 256), (512, 128)]


def network(edges, n, wh, p, l1, a1, a2, pool, m1, m2, d1, weights, emit):
    t1, t2, t3, t4, t5, t6, th = weights

    def rows(j, off, size):
        return pl.ds(pl.multiple_of((j + 4) * n + off, 16), size)

    def loop(count, cols, body):
        size = cols * n
        if count == cols:
            body(0, 0, size)
            return

        def step(i, carry):
            body(i * cols, i * size, size)
            return carry

        lax.fori_loop(0, count // cols, step, 0)

    def clear(ref, lead, first):
        for at in lead:
            for side, j, num in ((0, -first, first), (1, wh, first)):

                @pl.when(edges[side] > 0)
                def _(at=at, j=j, num=num):
                    ref[at + (rows(j, 0, num * n), slice(None))] = jnp.zeros((num * n, ref.shape[-1]), ref.dtype)

    both = [(0,), (1,)]
    four = [(q, h) for q in range(2) for h in range(2)]

    def near(q):
        return ((1, -1), (0, 0), (1, 0)) if q == 0 else ((0, 0), (1, 0), (0, 1))

    clear(p, both, 4)
    for q in range(2):
        j0 = -3 if q == 0 else -4
        size = (wh + 7) * n
        for s, (qs, dj) in enumerate(near(q)):
            l1[q, rows(j0, 0, size), 16 * s : 16 * s + 16] = p[qs, rows(j0 + dj, 0, size), :]

    c2, c6 = (wh + 6) // 2, wh // 2

    def relu(v):
        return jnp.maximum(v, 0.0).astype(BF)

    c1 = {15: 5, 39: 13}[wh + 7]

    def first(dj, off, size):
        for q in range(2):
            r = rows(-3 - q, off, size)
            x = l1[q, r, 0:48]
            for h in range(2):
                a1[q, h, r, :] = relu(dot(x, t1[h]))

    loop(wh + 7, c1, first)
    clear(a1, four, 4)

    def fine_conv(src, table, j0, off, size):
        ends = []
        for half, lanes in ((1, slice(0, 32)), (0, slice(224, 256))):
            ends += [src[q, half, rows(j0 + dj, off, size), lanes] for q, dj in ((1, -1), (0, 0), (1, 0), (0, 1))]
        extra = dot(jnp.concatenate(ends, axis=1), table[768:1024, :])
        low, high = extra[:, 0:128], extra[:, 128:256]
        lane = iota((size, 128), 1)
        outs = {}
        for q, h in four:
            own = [src[qs, h, rows(j0 + dj, off, size), :] for qs, dj in near(q)]
            acc = dot(jnp.concatenate(own, axis=1), table[0:768, :])
            left, right = acc[:, 0:128], acc[:, 128:256]
            if h == 0:
                right = right + jnp.where(lane >= 96, high if q == 0 else low, 0.0)
            else:
                left = left + jnp.where(lane < 32, low if q == 0 else high, 0.0)
            outs[q, h] = relu(left), relu(right)
        return outs

    def second(dj, off, size):
        outs = fine_conv(a1, t2, -3, off, size)
        r = rows(-3, off, size)
        for q, h in four:
            for i in range(2):
                a2[q, h, r, 128 * i : 128 * i + 128] = outs[q, h][i]
        even = iota((size, 128), 1) % 64 < 32
        for i in range(2):
            sums = [outs[0, h][i].astype(F32) + outs[1, h][i].astype(F32) for h in range(2)]
            sums = [sums[0] + pltpu.roll(sums[0], 96, 1), sums[1] + pltpu.roll(sums[1], 32, 1)]
            pool[r, 128 * i : 128 * i + 128] = (0.25 * jnp.where(even, sums[0], sums[1])).astype(BF)

    loop(wh + 6, c2, second)
    clear(a2, four, 3)
    clear(pool, [()], 3)

    def third(dj, off, size):
        x = jnp.concatenate([pool[rows(-2 + k, off, size), :] for k in (-1, 0, 1)], axis=1)
        y = relu(dot(x, t3[...]))
        for h in range(2):
            m1[h, rows(-2, off, size), :] = y[:, 256 * h : 256 * h + 256]

    loop(wh + 4, (wh + 4) // 2, third)
    clear(m1, both, 2)

    def fourth(dj, off, size):
        for h in range(2):
            other = slice(0, 64) if h == 0 else slice(192, 256)
            own = [m1[h, rows(-1 + k, off, size), :] for k in (-1, 0, 1)]
            edge = [m1[1 - h, rows(-1 + k, off, size), other] for k in (-1, 0, 1)]
            m2[h, rows(-1, off, size), :] = relu(dot(jnp.concatenate(own + edge, axis=1), t4[h]))

    loop(wh + 2, (wh + 2) // 2, fourth)
    clear(m2, both, 1)

    def fifth(dj, off, size):
        for q, h in four:
            j0 = -q
            other = slice(0, 32) if h == 0 else slice(224, 256)
            own = [a2[qs, h, rows(j0 + k, off, size), :] for qs, k in near(q)]
            edge = [a2[qs, 1 - h, rows(j0 + k, off, size), other] for qs, k in near(q)]
            other = slice(0, 64) if h == 0 else slice(192, 256)
            cells = (-1, 0) if q == 0 else (0, 1)
            own += [m2[h, rows(j0 + k, off, size), :] for k in cells]
            edge += [m2[1 - h, rows(j0 + k, off, size), other] for k in cells]
            d1[q, h, rows(j0, off, size), :] = relu(dot(jnp.concatenate(own + edge, axis=1), t5[q, h]))

    loop(wh + 1, {9: 3, 33: 11}[wh + 1], fifth)
    clear(d1, four, 1)

    def sixth(dj, off, size):
        outs = fine_conv(d1, t6, 0, off, size)
        for q in range(2):
            x = jnp.concatenate(outs[q, 0] + outs[q, 1], axis=1)
            emit(q, dj, c6, dot(x, th[...]))

    loop(wh, c6, sixth)


def unet_scratch(n, wh):
    m = (wh + 8) * n
    return [
        pltpu.VMEM((2, m, 16), BF),
        pltpu.VMEM((2, m, 128), BF),
        pltpu.VMEM((2, 2, m, 256), BF),
        pltpu.VMEM((2, 2, m, 256), BF),
        pltpu.VMEM((m, 256), BF),
        pltpu.VMEM((2, m, 256), BF),
        pltpu.VMEM((2, m, 256), BF),
        pltpu.VMEM((2, 2, m, 256), BF),
    ]


def xz_kernel(edges, v, *refs):
    held, out, tables, (vf, pf, hx), join, scratch = refs[0], refs[1], refs[2:7], refs[7:10], refs[10:12], refs[12:]
    weights = (*tables[:4], join[0], tables[4], join[1])
    n, wh = 16, 32
    for z in range(16):
        vf[16 * z : 16 * z + 16, :] = v[z].astype(F32)
    for y in range(16):
        turned = jnp.transpose(vf[pl.ds(y, 16, stride=16), :])
        pf[pl.ds(y, 80, stride=16), 0:16] = turned[0:80, :]
    p = scratch[0]
    for x in range(80):
        p[x % 2, 16 * (x // 2) : 16 * (x // 2) + 16, :] = pf[16 * x : 16 * x + 16, 0:16].astype(BF)

    build_tables(held, *tables)
    build_join(held, *join)

    def emit(q, j0, cols, head):
        for k in range(cols):
            at = pl.multiple_of((2 * (j0 + k) + q) * n, 16)
            hx[pl.ds(at, n), :] = head[k * n : k * n + n, :]

    network(edges, n, wh, *scratch, weights, emit)
    for y in range(16):
        out[y] = jnp.transpose(hx[pl.ds(y, 64, stride=16), :])[0:16, :]


def spread_kernel(place, v, row, out):
    t = place[0]
    lane = iota((16, 128), 1)
    pairs = []
    for z in range(8):
        low = pltpu.roll(v[z].astype(F32), 128 - HALO, 1)
        high = pltpu.roll(v[z + 8].astype(F32), 64 - HALO, 1)
        pairs.append(jnp.where(lane < 64, low, high))
    last = [jnp.concatenate([pairs[2 * k][8:], pairs[2 * k + 1][8:]], axis=0).astype(BF) for k in range(4)]
    first = [jnp.concatenate([pairs[2 * k][:8], pairs[2 * k + 1][:8]], axis=0).astype(BF) for k in range(4)]
    for p in range(16):
        for rows, cond in ((last, t < p), (first, t >= p)):

            @pl.when(cond)
            def _(p=p, rows=rows):
                for k in range(4):
                    out[p, k] = rows[k]

        out[p, 4] = row[...]


def yz_kernel(edges, xflags, v, shared, xz, *refs):
    tables, held, (out, vf, hf, hy, rf), join, scratch = refs[:5], refs[5], refs[6:11], refs[11:13], refs[13:]
    weights = (*tables[:4], join[0], tables[4], join[1])
    build_join(held, *join)
    n, wh = 64, 8
    p = scratch[0]
    tile, octet = edges[2], 8 * edges[3]
    for z in range(16):
        vf[16 * z : 16 * z + 16, :] = v[z].astype(F32)
    for side, source in ((0, jnp.maximum(tile - 1, 0)), (1, jnp.minimum(tile + 1, 15))):
        for k in range(4):
            both = shared[source, k].astype(F32)
            for i in range(2):
                at = 16 * (2 * k + i) + 8 * side
                hf[at : at + 8, :] = both[8 * i : 8 * i + 8, :]
    for k in range(32):
        at = slice(n * (k // 2), n * (k // 2) + n)
        if 8 <= k < 24:
            turned = jnp.transpose(vf[pl.ds(k - 8, 16, stride=16), :])
            p[k % 2, at, :] = turned[HALO : HALO + n, :].astype(BF)
        else:
            turned = jnp.transpose(hf[pl.ds(k if k < 8 else k - 16, 8, stride=16), :])
            p[k % 2, at, :] = jnp.concatenate([turned[0:n, :], turned[n:, :]], axis=1).astype(BF)

    def emit(q, j0, cols, head):
        for k in range(cols):
            at = pl.multiple_of((2 * (j0 + k) + q) * n, 16)
            hy[pl.ds(at, n), :] = head[k * n : k * n + n, :]

    network(edges, n, wh, *scratch, weights, emit)

    yes = sum(shared[octet + i, 4].astype(F32) for i in range(8))[0:1, 0:64] > 0.5
    for y in range(16):
        plane = pltpu.roll(vf[pl.ds(y, 16, stride=16), :], 128 - HALO, 1)[:, 0:64]
        yz = jnp.transpose(hy[64 * y : 64 * y + 64, :])[0:16, :]
        yz = jnp.where(yes, plane + yz, plane).astype(BF).astype(F32)
        xz_new = (plane + xz[y]).astype(BF).astype(F32)
        xz_new = jnp.where(xflags[y] > 0, xz_new, plane)
        rf[pl.ds(y, 16, stride=16), 0:64] = 0.5 * (xz_new + yz)
    for z in range(16):
        block = rf[16 * z : 16 * z + 16, 0:64].astype(BF)
        out[2 * (z // 2), z % 2] = block
        out[2 * (z // 2) + 1, z % 2] = block


def pack_kernel(side, v, out):
    for c, shift in ((0, HALO), (1, 1024 + HALO - 64)):

        @pl.when(side[0] == c)
        def _(shift=shift):
            for z in range(2):
                rolled = pltpu.roll(v[z].astype(F32), shift, 1).astype(BF)
                for s in range(8):
                    out[s, z] = rolled[:, 128 * s : 128 * s + 128]


def compute(xz_edges, yz_edges, xz_tissue, v, shared, raw):
    xz, *tables = pl.pallas_call(
        xz_kernel,
        out_shape=[jax.ShapeDtypeStruct((16, 16, 64), F32)] + [jax.ShapeDtypeStruct(s, BF) for s in TABLES],
        in_specs=[SMEM, VMEM, VMEM],
        out_specs=[VMEM] * 6,
        scratch_shapes=[pltpu.VMEM((256, 128), F32), pltpu.VMEM((1280, 128), F32), pltpu.VMEM((1024, 128), F32)]
        + [pltpu.VMEM(s, BF) for s in JOIN]
        + unet_scratch(16, 32),
        compiler_params=pltpu.CompilerParams(vmem_limit_bytes=24 << 20),
        cost_estimate=pl.CostEstimate(flops=6_000_000_000, bytes_accessed=6_000_000, transcendentals=0),
        name="xz",
    )(xz_edges, v, raw)
    return pl.pallas_call(
        yz_kernel,
        out_shape=jax.ShapeDtypeStruct((16, 2, 16, 64), BF),
        in_specs=[SMEM, SMEM] + [VMEM] * 9,
        out_specs=VMEM,
        scratch_shapes=[
            pltpu.VMEM((256, 128), F32),
            pltpu.VMEM((128, 128), F32),
            pltpu.VMEM((1024, 128), F32),
            pltpu.VMEM((256, 128), F32),
        ]
        + [pltpu.VMEM(s, BF) for s in JOIN]
        + unet_scratch(64, 8),
        compiler_params=pltpu.CompilerParams(vmem_limit_bytes=24 << 20),
        cost_estimate=pl.CostEstimate(flops=6_000_000_000, bytes_accessed=6_000_000, transcendentals=0),
        name="yz",
    )(yz_edges, xz_tissue, v, shared, xz, *tables, raw)


def per_device(volume, xz_tissue, yz_tissue, *weights):
    slab, tile, ch = lax.axis_index("slab"), lax.axis_index("tile"), lax.axis_index("ch")
    packed = pl.pallas_call(
        pack_kernel,
        out_shape=jax.ShapeDtypeStruct((8, 2, 16, 128), BF),
        in_specs=[SMEM, VMEM],
        out_specs=VMEM,
        name="pack",
    )(ch[None].astype(jnp.int32), volume)
    moved = lax.all_to_all(packed, "slab", split_axis=0, concat_axis=0, tiled=True)
    v = moved.reshape(16, 16, 128)
    raw = stage(prepare(*weights))

    mine = (jnp.arange(128) // 8 == tile % 8)[None, :]
    row = jnp.where(mine, jnp.tile(yz_tissue, 16)[None, :], 0).astype(BF)
    shared = pl.pallas_call(
        spread_kernel,
        out_shape=jax.ShapeDtypeStruct((16, 5, 16, 128), BF),
        in_specs=[SMEM, VMEM, VMEM],
        out_specs=VMEM,
        compiler_params=pltpu.CompilerParams(vmem_limit_bytes=8 << 20),
        name="spread",
    )(tile[None].astype(jnp.int32), v, jnp.broadcast_to(row, (16, 128)))
    shared = lax.all_to_all(shared, "tile", split_axis=0, concat_axis=0, tiled=True)

    window = 2 * slab + ch
    xz_edges = jnp.stack([window == 0, window == 15]).astype(jnp.int32)
    yz_edges = jnp.stack([tile == 0, tile == 15, tile, ch]).astype(jnp.int32)

    block = compute(xz_edges, yz_edges, xz_tissue, v, shared, raw)
    back = lax.all_to_all(block, ("slab", "ch"), split_axis=0, concat_axis=0, tiled=True)
    return jnp.transpose(back, (1, 2, 0, 3)).reshape(2, 16, 1024)


def solution(mesh):
    return jax.shard_map(
        per_device,
        mesh=mesh,
        in_specs=(P("slab", "tile", None), P("tile"), P(("slab", "tile"))) + (P(),) * 7,
        out_specs=P("slab", "tile", None),
        check_vma=False,
    )
```

```python
import jax
import jax.numpy as jnp
from jax import lax
from jax.experimental import pallas as pl
from jax.experimental.pallas import tpu as pltpu
from jax.sharding import PartitionSpec as P

BF = jnp.bfloat16
F32 = jnp.float32
SMEM = pl.BlockSpec(memory_space=pltpu.SMEM)
VMEM = pl.BlockSpec(memory_space=pltpu.VMEM)
HALO = 8


def iota(shape, dim):
    return lax.broadcasted_iota(jnp.int32, shape, dim)


def dot(a, b):
    return jnp.dot(a, b, preferred_element_type=F32)


def spread(tap, cells, out_first):
    outs = tap.shape[0 if out_first else 1]
    shape = (outs, cells * outs)
    pick = (iota(shape, 0) == iota(shape, 1) % outs).astype(F32).astype(BF)
    dims = (((0 if out_first else 1,), (0,)), ((), ()))
    return lax.dot_general(tap, pick, dims, preferred_element_type=F32)


def stack_rows(tap, cells):
    return jnp.concatenate([tap] * cells, axis=0)


def taps_of(held, first, last):
    return lambda t, lo, hi: held[t, first:last, lo:hi]


def fine(src, lo, hi, base, own, edges, merged):
    row, lane = iota((256, 256), 0) // 32, iota((256, 256), 1) // 32
    g = [spread(src(t, lo, hi), 8, True) for t in range(9)]
    edge = iota((32, 256), 1) // 32
    for s in range(3):
        tile = jnp.zeros((256, 256), F32)
        for r in range(3):
            tile = jnp.where(row == lane + (r - 1), stack_rows(g[3 * r + s], 8), tile)
        tile = tile.astype(BF)
        for d in own:
            d[256 * s : 256 * s + 256, :] = tile
        for h, near, taps in ((0, 7, g[6 + s]), (1, 0, g[s])):
            for d in edges:
                d[h, base + 32 * s : base + 32 * s + 32, :] = jnp.where(edge == near, taps, 0.0).astype(BF)
    for d in merged:
        for h in range(2):
            for k in range(4):
                tile = jnp.zeros((32, 256), F32)
                for q in range(2):
                    s = k - q
                    if 0 <= s < 3:
                        near = (7, 3)[q] if h == 0 else (0, 4)[q]
                        tile = jnp.where(edge == near, g[6 + s] if h == 0 else g[s], tile)
                d[128 * h + 32 * k : 128 * h + 32 * k + 32, :] = tile.astype(BF)


def build_tables(held, t1, t2, t3, t4):
    w2, w3, w4 = taps_of(held, 0, 32), taps_of(held, 32, 64), taps_of(held, 64, 128)

    fine(w2, 0, 32, 0, [t2.at[0:768]], [], [t2.at[768:1024]])

    row, lane = iota((16, 256), 0), iota((16, 256), 1) // 32
    first = spread(held[9, 0:16, 0:32], 8, False)
    for s in range(3):
        g = [first[3 * r + s : 3 * r + s + 1, :] for r in range(3)]
        for h in range(2):
            tile = jnp.zeros((16, 256), F32)
            for r in range(3):
                tile = jnp.where(row == lane + 8 * h + (r - 1), jnp.broadcast_to(g[r], (16, 256)), tile)
            t1[h, 16 * s : 16 * s + 16, :] = tile.astype(BF)

    row, lane = iota((256, 256), 0) // 32, iota((256, 256), 1) // 64
    row = row // 2 + 4 * (row % 2)
    g = [spread(w3(t, 0, 64), 4, False) for t in range(9)]
    for s in range(3):
        for h in range(2):
            tile = jnp.zeros((256, 256), F32)
            for r in range(3):
                tile = jnp.where(row == lane + 4 * h + (r - 1), stack_rows(g[3 * r + s], 8), tile)
            t3[256 * s : 256 * s + 256, 256 * h : 256 * h + 256] = tile.astype(BF)

    row, lane = iota((256, 256), 0) // 64, iota((256, 256), 1) // 64
    edge = iota((64, 256), 1) // 64
    g = [spread(w4(t, 0, 64), 4, True) for t in range(9)]
    for s in range(3):
        tile = jnp.zeros((256, 256), F32)
        for r in range(3):
            tile = jnp.where(row == lane + (r - 1), stack_rows(g[3 * r + s], 4), tile)
        tile = tile.astype(BF)
        for h in range(2):
            t4[h, 256 * s : 256 * s + 256, :] = tile
        t4[0, 768 + 64 * s : 832 + 64 * s, :] = jnp.where(edge == 3, g[6 + s], 0.0).astype(BF)
        t4[1, 768 + 64 * s : 832 + 64 * s, :] = jnp.where(edge == 0, g[s], 0.0).astype(BF)


def build_join(held, t5, t6, th):
    w5, w6 = taps_of(held, 128, 160), taps_of(held, 160, 192)
    fine(w6, 0, 32, 0, [t6.at[0:768]], [], [t6.at[768:1024]])
    fine(w5, 64, 96, 1280, [t5.at[q, h] for q in range(2) for h in range(2)], [t5.at[0], t5.at[1]], [])

    row, lane = iota((256, 256), 0) // 64, iota((256, 256), 1) // 32
    edge = iota((64, 256), 1) // 32
    g = [spread(w5(t, 0, 64), 8, True) for t in range(9)]
    for q in range(2):
        groups = ((0,), (1, 2)) if q == 0 else ((0, 1), (2,))
        for i, taps in enumerate(groups):
            tile = jnp.zeros((256, 256), F32)
            for r in range(3):
                part = sum(g[3 * r + s] for s in taps)
                hit = row == ((lane + (r - 1) + 2) // 2 - 1)
                tile = tile + jnp.where(hit, stack_rows(part, 4), 0.0)
            tile = tile.astype(BF)
            for h in range(2):
                t5[q, h, 768 + 256 * i : 1024 + 256 * i, :] = tile
            below = sum(g[6 + s] for s in taps)
            above = sum(g[s] for s in taps)
            t5[q, 0, 1376 + 64 * i : 1440 + 64 * i, :] = jnp.where(edge == 7, below, 0.0).astype(BF)
            t5[q, 1, 1376 + 64 * i : 1440 + 64 * i, :] = jnp.where(edge == 0, above, 0.0).astype(BF)

    row, lane = iota((512, 128), 0), iota((512, 128), 1)
    pick = (iota((512, 32), 0) % 32 == iota((512, 32), 1)).astype(F32)
    column = jnp.sum(pick * held[9, 16:32, 0:32].astype(F32)[0:1], axis=1, keepdims=True)
    th[...] = jnp.where(row // 32 == lane, column, 0.0).astype(BF)


def stage_kernel(w1, w2, w3, w4, w5, w6, wo, out):
    for t in range(9):
        out[t, 0:32, 0:32] = w2[t]
        out[t, 32:64, 0:64] = w3[t]
        out[t, 64:128, 0:64] = w4[t]
        out[t, 128:160, 0:96] = w5[t]
        out[t, 160:192, 0:32] = w6[t]
    out[9, 0:32, :] = jnp.zeros((32, 128), BF)
    out[9, 0:9, 0:32] = w1[...]
    out[9, 16:17, 0:32] = wo[...]


def stage(raw):
    return pl.pallas_call(
        stage_kernel,
        out_shape=jax.ShapeDtypeStruct((10, 192, 128), BF),
        in_specs=[VMEM] * 7,
        out_specs=VMEM,
        name="stage",
    )(*raw)


def prepare(w1, w2, w3, w4, w5, w6, wo):
    taps = [jnp.transpose(w1[:, :, 0])] + [jnp.transpose(w, (1, 0, 2)) for w in (w2, w3, w4, w5, w6)]
    taps[2] = jnp.transpose(w3, (1, 2, 0))
    return taps + [wo[None, :]]


TABLES = [(2, 48, 256), (1024, 256), (768, 512), (2, 960, 256)]
JOIN = [(2, 2, 1504, 256), (1024, 256), (512, 128)]


def network(edges, n, wh, p, l1, a1, a2, pool, m1, m2, d1, weights, emit):
    t1, t2, t3, t4, t5, t6, th = weights

    def rows(j, off, size):
        return pl.ds(pl.multiple_of((j + 4) * n + off, 16), size)

    def loop(count, cols, body):
        size = cols * n
        if count == cols:
            body(0, 0, size)
            return

        def step(i, carry):
            body(i * cols, i * size, size)
            return carry

        lax.fori_loop(0, count // cols, step, 0)

    def clear(ref, lead, first):
        for at in lead:
            for side, j, num in ((0, -first, first), (1, wh, first)):

                @pl.when(edges[side] > 0)
                def _(at=at, j=j, num=num):
                    ref[at + (rows(j, 0, num * n), slice(None))] = jnp.zeros((num * n, ref.shape[-1]), ref.dtype)

    both = [(0,), (1,)]
    four = [(q, h) for q in range(2) for h in range(2)]

    def near(q):
        return ((1, -1), (0, 0), (1, 0)) if q == 0 else ((0, 0), (1, 0), (0, 1))

    clear(p, both, 4)
    for q in range(2):
        j0 = -3 if q == 0 else -4
        size = (wh + 7) * n
        for s, (qs, dj) in enumerate(near(q)):
            l1[q, rows(j0, 0, size), 16 * s : 16 * s + 16] = p[qs, rows(j0 + dj, 0, size), :]

    c2, c6 = (wh + 6) // 2, wh // 2

    def relu(v):
        return jnp.maximum(v, 0.0).astype(BF)

    c1 = {15: 5, 39: 13}[wh + 7]

    def first(dj, off, size):
        for q in range(2):
            r = rows(-3 - q, off, size)
            x = l1[q, r, 0:48]
            for h in range(2):
                a1[q, h, r, :] = relu(dot(x, t1[h]))

    loop(wh + 7, c1, first)
    clear(a1, four, 4)

    def fine_conv(src, table, j0, off, size):
        ends = []
        for half, lanes in ((1, slice(0, 32)), (0, slice(224, 256))):
            ends += [src[q, half, rows(j0 + dj, off, size), lanes] for q, dj in ((1, -1), (0, 0), (1, 0), (0, 1))]
        extra = dot(jnp.concatenate(ends, axis=1), table[768:1024, :])
        low, high = extra[:, 0:128], extra[:, 128:256]
        lane = iota((size, 128), 1)
        outs = {}
        for q, h in four:
            own = [src[qs, h, rows(j0 + dj, off, size), :] for qs, dj in near(q)]
            acc = dot(jnp.concatenate(own, axis=1), table[0:768, :])
            left, right = acc[:, 0:128], acc[:, 128:256]
            if h == 0:
                right = right + jnp.where(lane >= 96, high if q == 0 else low, 0.0)
            else:
                left = left + jnp.where(lane < 32, low if q == 0 else high, 0.0)
            outs[q, h] = relu(left), relu(right)
        return outs

    def second(dj, off, size):
        outs = fine_conv(a1, t2, -3, off, size)
        r = rows(-3, off, size)
        for q, h in four:
            for i in range(2):
                a2[q, h, r, 128 * i : 128 * i + 128] = outs[q, h][i]
        even = iota((size, 128), 1) % 64 < 32
        for i in range(2):
            sums = [outs[0, h][i].astype(F32) + outs[1, h][i].astype(F32) for h in range(2)]
            sums = [sums[0] + pltpu.roll(sums[0], 96, 1), sums[1] + pltpu.roll(sums[1], 32, 1)]
            pool[r, 128 * i : 128 * i + 128] = (0.25 * jnp.where(even, sums[0], sums[1])).astype(BF)

    loop(wh + 6, c2, second)
    clear(a2, four, 3)
    clear(pool, [()], 3)

    def third(dj, off, size):
        x = jnp.concatenate([pool[rows(-2 + k, off, size), :] for k in (-1, 0, 1)], axis=1)
        y = relu(dot(x, t3[...]))
        for h in range(2):
            m1[h, rows(-2, off, size), :] = y[:, 256 * h : 256 * h + 256]

    loop(wh + 4, (wh + 4) // 2, third)
    clear(m1, both, 2)

    def fourth(dj, off, size):
        for h in range(2):
            other = slice(0, 64) if h == 0 else slice(192, 256)
            own = [m1[h, rows(-1 + k, off, size), :] for k in (-1, 0, 1)]
            edge = [m1[1 - h, rows(-1 + k, off, size), other] for k in (-1, 0, 1)]
            m2[h, rows(-1, off, size), :] = relu(dot(jnp.concatenate(own + edge, axis=1), t4[h]))

    loop(wh + 2, (wh + 2) // 2, fourth)
    clear(m2, both, 1)

    def fifth(dj, off, size):
        for q, h in four:
            j0 = -q
            other = slice(0, 32) if h == 0 else slice(224, 256)
            own = [a2[qs, h, rows(j0 + k, off, size), :] for qs, k in near(q)]
            edge = [a2[qs, 1 - h, rows(j0 + k, off, size), other] for qs, k in near(q)]
            other = slice(0, 64) if h == 0 else slice(192, 256)
            cells = (-1, 0) if q == 0 else (0, 1)
            own += [m2[h, rows(j0 + k, off, size), :] for k in cells]
            edge += [m2[1 - h, rows(j0 + k, off, size), other] for k in cells]
            d1[q, h, rows(j0, off, size), :] = relu(dot(jnp.concatenate(own + edge, axis=1), t5[q, h]))

    loop(wh + 1, {9: 3, 33: 11}[wh + 1], fifth)
    clear(d1, four, 1)

    def sixth(dj, off, size):
        outs = fine_conv(d1, t6, 0, off, size)
        for q in range(2):
            x = jnp.concatenate(outs[q, 0] + outs[q, 1], axis=1)
            emit(q, dj, c6, dot(x, th[...]))

    loop(wh, c6, sixth)


def unet_scratch(n, wh):
    m = (wh + 8) * n
    return [
        pltpu.VMEM((2, m, 16), BF),
        pltpu.VMEM((2, m, 128), BF),
        pltpu.VMEM((2, 2, m, 256), BF),
        pltpu.VMEM((2, 2, m, 256), BF),
        pltpu.VMEM((m, 256), BF),
        pltpu.VMEM((2, m, 256), BF),
        pltpu.VMEM((2, m, 256), BF),
        pltpu.VMEM((2, 2, m, 256), BF),
    ]


def xz_kernel(edges, v, *refs):
    held, out, tables, (vf, pf, hx), join, scratch = refs[0], refs[1], refs[2:6], refs[6:9], refs[9:12], refs[12:]
    weights = (*tables, *join)
    n, wh = 16, 32
    for z in range(16):
        vf[16 * z : 16 * z + 16, :] = v[z].astype(F32)
    for y in range(16):
        turned = jnp.transpose(vf[pl.ds(y, 16, stride=16), :])
        pf[pl.ds(y, 80, stride=16), 0:16] = turned[0:80, :]
    p = scratch[0]
    for x in range(80):
        p[x % 2, 16 * (x // 2) : 16 * (x // 2) + 16, :] = pf[16 * x : 16 * x + 16, 0:16].astype(BF)

    build_tables(held, *tables)
    build_join(held, *join)

    def emit(q, j0, cols, head):
        for k in range(cols):
            at = pl.multiple_of((2 * (j0 + k) + q) * n, 16)
            hx[pl.ds(at, n), :] = head[k * n : k * n + n, :]

    network(edges, n, wh, *scratch, weights, emit)
    for y in range(16):
        out[y] = jnp.transpose(hx[pl.ds(y, 64, stride=16), :])[0:16, :]


def spread_kernel(place, v, row, out):
    t = place[0]
    lane = iota((16, 128), 1)
    pairs = []
    for z in range(8):
        low = pltpu.roll(v[z].astype(F32), 128 - HALO, 1)
        high = pltpu.roll(v[z + 8].astype(F32), 64 - HALO, 1)
        pairs.append(jnp.where(lane < 64, low, high))
    last = [jnp.concatenate([pairs[2 * k][8:], pairs[2 * k + 1][8:]], axis=0).astype(BF) for k in range(4)]
    first = [jnp.concatenate([pairs[2 * k][:8], pairs[2 * k + 1][:8]], axis=0).astype(BF) for k in range(4)]
    for p in range(16):
        for rows, cond in ((last, t < p), (first, t >= p)):

            @pl.when(cond)
            def _(p=p, rows=rows):
                for k in range(4):
                    out[p, k] = rows[k]

        out[p, 4] = row[...]


def yz_kernel(edges, v, shared, xz, *refs):
    tables, held, (out, vf, hf, hy, rf), join, scratch = refs[:4], refs[4], refs[5:10], refs[10:13], refs[13:]
    weights = (*tables, *join)
    build_join(held, *join)
    n, wh = 64, 8
    p = scratch[0]
    tile, octet = edges[2], 8 * edges[3]
    for z in range(16):
        vf[16 * z : 16 * z + 16, :] = v[z].astype(F32)
    for side, source in ((0, jnp.maximum(tile - 1, 0)), (1, jnp.minimum(tile + 1, 15))):
        for k in range(4):
            both = shared[source, k].astype(F32)
            for i in range(2):
                at = 16 * (2 * k + i) + 8 * side
                hf[at : at + 8, :] = both[8 * i : 8 * i + 8, :]
    for k in range(32):
        at = slice(n * (k // 2), n * (k // 2) + n)
        if 8 <= k < 24:
            turned = jnp.transpose(vf[pl.ds(k - 8, 16, stride=16), :])
            p[k % 2, at, :] = turned[HALO : HALO + n, :].astype(BF)
        else:
            turned = jnp.transpose(hf[pl.ds(k if k < 8 else k - 16, 8, stride=16), :])
            p[k % 2, at, :] = jnp.concatenate([turned[0:n, :], turned[n:, :]], axis=1).astype(BF)

    def emit(q, j0, cols, head):
        for k in range(cols):
            at = pl.multiple_of((2 * (j0 + k) + q) * n, 16)
            hy[pl.ds(at, n), :] = head[k * n : k * n + n, :]

    network(edges, n, wh, *scratch, weights, emit)

    yes = sum(shared[octet + i, 4].astype(F32) for i in range(8))[0:1, 0:64] > 0.5
    for y in range(16):
        plane = pltpu.roll(vf[pl.ds(y, 16, stride=16), :], 128 - HALO, 1)[:, 0:64]
        yz = jnp.transpose(hy[64 * y : 64 * y + 64, :])[0:16, :]
        yz = jnp.where(yes, plane + yz, plane).astype(BF).astype(F32)
        xz_new = (plane + xz[y]).astype(BF).astype(F32)
        xz_new = jnp.where(edges[4 + y] > 0, xz_new, plane)
        rf[pl.ds(y, 16, stride=16), 0:64] = 0.5 * (xz_new + yz)
    for z in range(16):
        block = rf[16 * z : 16 * z + 16, 0:64].astype(BF)
        out[2 * (z // 2), z % 2] = block
        out[2 * (z // 2) + 1, z % 2] = block


def pack_kernel(side, v, out):
    for c, shift in ((0, HALO), (1, 1024 + HALO - 64)):

        @pl.when(side[0] == c)
        def _(shift=shift):
            for z in range(2):
                rolled = pltpu.roll(v[z].astype(F32), shift, 1).astype(BF)
                for s in range(8):
                    out[s, z] = rolled[:, 128 * s : 128 * s + 128]


def compute(xz_edges, yz_edges, v, shared, raw):
    xz, *tables = pl.pallas_call(
        xz_kernel,
        out_shape=[jax.ShapeDtypeStruct((16, 16, 64), F32)] + [jax.ShapeDtypeStruct(s, BF) for s in TABLES],
        in_specs=[SMEM, VMEM, VMEM],
        out_specs=[VMEM] * 5,
        scratch_shapes=[pltpu.VMEM((256, 128), F32), pltpu.VMEM((1280, 128), F32), pltpu.VMEM((1024, 128), F32)]
        + [pltpu.VMEM(s, BF) for s in JOIN]
        + unet_scratch(16, 32),
        compiler_params=pltpu.CompilerParams(vmem_limit_bytes=24 << 20),
        cost_estimate=pl.CostEstimate(flops=6_000_000_000, bytes_accessed=6_000_000, transcendentals=0),
        name="xz",
    )(xz_edges, v, raw)
    return pl.pallas_call(
        yz_kernel,
        out_shape=jax.ShapeDtypeStruct((16, 2, 16, 64), BF),
        in_specs=[SMEM] + [VMEM] * 8,
        out_specs=VMEM,
        scratch_shapes=[
            pltpu.VMEM((256, 128), F32),
            pltpu.VMEM((128, 128), F32),
            pltpu.VMEM((1024, 128), F32),
            pltpu.VMEM((256, 128), F32),
        ]
        + [pltpu.VMEM(s, BF) for s in JOIN]
        + unet_scratch(64, 8),
        compiler_params=pltpu.CompilerParams(vmem_limit_bytes=24 << 20),
        cost_estimate=pl.CostEstimate(flops=6_000_000_000, bytes_accessed=6_000_000, transcendentals=0),
        name="yz",
    )(yz_edges, v, shared, xz, *tables, raw)


def per_device(volume, xz_tissue, yz_tissue, *weights):
    slab, tile, ch = lax.axis_index("slab"), lax.axis_index("tile"), lax.axis_index("ch")
    packed = pl.pallas_call(
        pack_kernel,
        out_shape=jax.ShapeDtypeStruct((8, 2, 16, 128), BF),
        in_specs=[SMEM, VMEM],
        out_specs=VMEM,
        name="pack",
    )(ch[None].astype(jnp.int32), volume)
    moved = lax.all_to_all(packed, "slab", split_axis=0, concat_axis=0, tiled=True)
    v = moved.reshape(16, 16, 128)
    raw = stage(prepare(*weights))

    mine = (jnp.arange(128) // 8 == tile % 8)[None, :]
    row = jnp.where(mine, jnp.tile(yz_tissue, 16)[None, :], 0).astype(BF)
    shared = pl.pallas_call(
        spread_kernel,
        out_shape=jax.ShapeDtypeStruct((16, 5, 16, 128), BF),
        in_specs=[SMEM, VMEM, VMEM],
        out_specs=VMEM,
        compiler_params=pltpu.CompilerParams(vmem_limit_bytes=8 << 20),
        name="spread",
    )(tile[None].astype(jnp.int32), v, jnp.broadcast_to(row, (16, 128)))
    shared = lax.all_to_all(shared, "tile", split_axis=0, concat_axis=0, tiled=True)

    window = 2 * slab + ch
    xz_edges = jnp.stack([window == 0, window == 15]).astype(jnp.int32)
    yz_edges = jnp.stack([tile == 0, tile == 15, tile, ch]).astype(jnp.int32)
    yz_edges = jnp.concatenate([yz_edges, xz_tissue])

    block = compute(xz_edges, yz_edges, v, shared, raw)
    back = lax.all_to_all(block, ("slab", "ch"), split_axis=0, concat_axis=0, tiled=True)
    return jnp.transpose(back, (1, 2, 0, 3)).reshape(2, 16, 1024)


def solution(mesh):
    return jax.shard_map(
        per_device,
        mesh=mesh,
        in_specs=(P("slab", "tile", None), P("tile"), P(("slab", "tile"))) + (P(),) * 7,
        out_specs=P("slab", "tile", None),
        check_vma=False,
    )
```

```python
import jax
import jax.numpy as jnp
from jax import lax
from jax.experimental import pallas as pl
from jax.experimental.pallas import tpu as pltpu
from jax.sharding import PartitionSpec as P

BF = jnp.bfloat16
F32 = jnp.float32
SMEM = pl.BlockSpec(memory_space=pltpu.SMEM)
VMEM = pl.BlockSpec(memory_space=pltpu.VMEM)
HALO = 8


def iota(shape, dim):
    return lax.broadcasted_iota(jnp.int32, shape, dim)


def dot(a, b):
    return jnp.dot(a, b, preferred_element_type=F32)


def spread(tap, cells, out_first):
    outs = tap.shape[0 if out_first else 1]
    shape = (outs, cells * outs)
    pick = (iota(shape, 0) == iota(shape, 1) % outs).astype(F32).astype(BF)
    dims = (((0 if out_first else 1,), (0,)), ((), ()))
    return lax.dot_general(tap, pick, dims, preferred_element_type=F32)


def stack_rows(tap, cells):
    return jnp.concatenate([tap] * cells, axis=0)


def taps_of(held, first, last):
    return lambda t, lo, hi: held[t, first:last, lo:hi]


def fine(src, lo, hi, base, own, edges, merged):
    row, lane = iota((256, 256), 0) // 32, iota((256, 256), 1) // 32
    g = [spread(src(t, lo, hi), 8, True) for t in range(9)]
    edge = iota((32, 256), 1) // 32
    for s in range(3):
        tile = jnp.zeros((256, 256), F32)
        for r in range(3):
            tile = jnp.where(row == lane + (r - 1), stack_rows(g[3 * r + s], 8), tile)
        tile = tile.astype(BF)
        for d in own:
            d[256 * s : 256 * s + 256, :] = tile
        for h, near, taps in ((0, 7, g[6 + s]), (1, 0, g[s])):
            for d in edges:
                d[h, base + 32 * s : base + 32 * s + 32, :] = jnp.where(edge == near, taps, 0.0).astype(BF)
    for d in merged:
        for h in range(2):
            for k in range(4):
                tile = jnp.zeros((32, 256), F32)
                for q in range(2):
                    s = k - q
                    if 0 <= s < 3:
                        near = (7, 3)[q] if h == 0 else (0, 4)[q]
                        tile = jnp.where(edge == near, g[6 + s] if h == 0 else g[s], tile)
                d[128 * h + 32 * k : 128 * h + 32 * k + 32, :] = tile.astype(BF)


def build_tables(held, t1, t2, t3, t4):
    w2, w3, w4 = taps_of(held, 0, 32), taps_of(held, 32, 64), taps_of(held, 64, 128)

    fine(w2, 0, 32, 0, [t2.at[0:768]], [], [t2.at[768:1024]])

    row, lane = iota((16, 256), 0), iota((16, 256), 1) // 32
    first = spread(held[9, 0:16, 0:32], 8, False)
    for s in range(3):
        g = [first[3 * r + s : 3 * r + s + 1, :] for r in range(3)]
        for h in range(2):
            tile = jnp.zeros((16, 256), F32)
            for r in range(3):
                tile = jnp.where(row == lane + 8 * h + (r - 1), jnp.broadcast_to(g[r], (16, 256)), tile)
            t1[h, 16 * s : 16 * s + 16, :] = tile.astype(BF)

    row, lane = iota((256, 256), 0) // 32, iota((256, 256), 1) // 64
    row = row // 2 + 4 * (row % 2)
    g = [spread(w3(t, 0, 64), 4, False) for t in range(9)]
    for s in range(3):
        for h in range(2):
            tile = jnp.zeros((256, 256), F32)
            for r in range(3):
                tile = jnp.where(row == lane + 4 * h + (r - 1), stack_rows(g[3 * r + s], 8), tile)
            t3[256 * s : 256 * s + 256, 256 * h : 256 * h + 256] = tile.astype(BF)

    row, lane = iota((256, 256), 0) // 64, iota((256, 256), 1) // 64
    edge = iota((64, 256), 1) // 64
    g = [spread(w4(t, 0, 64), 4, True) for t in range(9)]
    for s in range(3):
        tile = jnp.zeros((256, 256), F32)
        for r in range(3):
            tile = jnp.where(row == lane + (r - 1), stack_rows(g[3 * r + s], 4), tile)
        tile = tile.astype(BF)
        for h in range(2):
            t4[h, 256 * s : 256 * s + 256, :] = tile
        t4[0, 768 + 64 * s : 832 + 64 * s, :] = jnp.where(edge == 3, g[6 + s], 0.0).astype(BF)
        t4[1, 768 + 64 * s : 832 + 64 * s, :] = jnp.where(edge == 0, g[s], 0.0).astype(BF)


def build_join(held, t5, t6, th):
    w5, w6 = taps_of(held, 128, 160), taps_of(held, 160, 192)
    fine(w6, 0, 32, 0, [t6.at[0:768]], [], [t6.at[768:1024]])
    fine(w5, 64, 96, 1280, [t5.at[q, h] for q in range(2) for h in range(2)], [t5.at[0], t5.at[1]], [])

    row, lane = iota((256, 256), 0) // 64, iota((256, 256), 1) // 32
    edge = iota((64, 256), 1) // 32
    g = [spread(w5(t, 0, 64), 8, True) for t in range(9)]
    for q in range(2):
        groups = ((0,), (1, 2)) if q == 0 else ((0, 1), (2,))
        for i, taps in enumerate(groups):
            tile = jnp.zeros((256, 256), F32)
            for r in range(3):
                part = sum(g[3 * r + s] for s in taps)
                hit = row == ((lane + (r - 1) + 2) // 2 - 1)
                tile = tile + jnp.where(hit, stack_rows(part, 4), 0.0)
            tile = tile.astype(BF)
            for h in range(2):
                t5[q, h, 768 + 256 * i : 1024 + 256 * i, :] = tile
            below = sum(g[6 + s] for s in taps)
            above = sum(g[s] for s in taps)
            t5[q, 0, 1376 + 64 * i : 1440 + 64 * i, :] = jnp.where(edge == 7, below, 0.0).astype(BF)
            t5[q, 1, 1376 + 64 * i : 1440 + 64 * i, :] = jnp.where(edge == 0, above, 0.0).astype(BF)

    row, lane = iota((512, 128), 0), iota((512, 128), 1)
    pick = (iota((512, 32), 0) % 32 == iota((512, 32), 1)).astype(F32)
    column = jnp.sum(pick * held[9, 16:32, 0:32].astype(F32)[0:1], axis=1, keepdims=True)
    th[...] = jnp.where(row // 32 == lane, column, 0.0).astype(BF)


def stage_kernel(w1, w2, w3, w4, w5, w6, wo, out):
    for t in range(9):
        out[t, 0:32, 0:32] = w2[t]
        out[t, 32:64, 0:64] = w3[t]
        out[t, 64:128, 0:64] = w4[t]
        out[t, 128:160, 0:96] = w5[t]
        out[t, 160:192, 0:32] = w6[t]
    out[9, 0:32, :] = jnp.zeros((32, 128), BF)
    out[9, 0:9, 0:32] = w1[...]
    out[9, 16:17, 0:32] = wo[...]


def stage(raw):
    return pl.pallas_call(
        stage_kernel,
        out_shape=jax.ShapeDtypeStruct((10, 192, 128), BF),
        in_specs=[VMEM] * 7,
        out_specs=VMEM,
        name="stage",
    )(*raw)


def prepare(w1, w2, w3, w4, w5, w6, wo):
    taps = [jnp.transpose(w1[:, :, 0])] + [jnp.transpose(w, (1, 0, 2)) for w in (w2, w3, w4, w5, w6)]
    taps[2] = jnp.transpose(w3, (1, 2, 0))
    return taps + [wo[None, :]]


TABLES = [(2, 48, 256), (1024, 256), (768, 512), (2, 960, 256)]
JOIN = [(2, 2, 1504, 256), (1024, 256), (512, 128)]


def network(edges, n, wh, p, l1, a1, a2, pool, m1, m2, d1, weights, emit):
    t1, t2, t3, t4, t5, t6, th = weights

    def rows(j, off, size):
        return pl.ds(pl.multiple_of((j + 4) * n + off, 16), size)

    def loop(count, cols, body):
        size = cols * n
        if count == cols:
            body(0, 0, size)
            return

        def step(i, carry):
            body(i * cols, i * size, size)
            return carry

        lax.fori_loop(0, count // cols, step, 0)

    def clear(ref, lead, first):
        for at in lead:
            for side, j, num in ((0, -first, first), (1, wh, first)):

                @pl.when(edges[side] > 0)
                def _(at=at, j=j, num=num):
                    ref[at + (rows(j, 0, num * n), slice(None))] = jnp.zeros((num * n, ref.shape[-1]), ref.dtype)

    both = [(0,), (1,)]
    four = [(q, h) for q in range(2) for h in range(2)]

    def near(q):
        return ((1, -1), (0, 0), (1, 0)) if q == 0 else ((0, 0), (1, 0), (0, 1))

    clear(p, both, 4)
    for q in range(2):
        j0 = -3 if q == 0 else -4
        size = (wh + 7) * n
        for s, (qs, dj) in enumerate(near(q)):
            l1[q, rows(j0, 0, size), 16 * s : 16 * s + 16] = p[qs, rows(j0 + dj, 0, size), :]

    c2, c6 = (wh + 6) // 2, wh // 2

    def relu(v):
        return jnp.maximum(v, 0.0).astype(BF)

    c1 = {15: 5, 39: 13}[wh + 7]

    def first(dj, off, size):
        for q in range(2):
            r = rows(-3 - q, off, size)
            x = l1[q, r, 0:48]
            for h in range(2):
                a1[q, h, r, :] = relu(dot(x, t1[h]))

    loop(wh + 7, c1, first)
    clear(a1, four, 4)

    def fine_conv(src, table, j0, off, size):
        ends = []
        for half, lanes in ((1, slice(0, 32)), (0, slice(224, 256))):
            ends += [src[q, half, rows(j0 + dj, off, size), lanes] for q, dj in ((1, -1), (0, 0), (1, 0), (0, 1))]
        extra = dot(jnp.concatenate(ends, axis=1), table[768:1024, :])
        low, high = extra[:, 0:128], extra[:, 128:256]
        lane = iota((size, 128), 1)
        outs = {}
        for q, h in four:
            own = [src[qs, h, rows(j0 + dj, off, size), :] for qs, dj in near(q)]
            acc = dot(jnp.concatenate(own, axis=1), table[0:768, :])
            left, right = acc[:, 0:128], acc[:, 128:256]
            if h == 0:
                right = right + jnp.where(lane >= 96, high if q == 0 else low, 0.0)
            else:
                left = left + jnp.where(lane < 32, low if q == 0 else high, 0.0)
            outs[q, h] = relu(left), relu(right)
        return outs

    def second(dj, off, size):
        outs = fine_conv(a1, t2, -3, off, size)
        r = rows(-3, off, size)
        for q, h in four:
            for i in range(2):
                a2[q, h, r, 128 * i : 128 * i + 128] = outs[q, h][i]
        even = iota((size, 128), 1) % 64 < 32
        for i in range(2):
            sums = [outs[0, h][i].astype(F32) + outs[1, h][i].astype(F32) for h in range(2)]
            sums = [sums[0] + pltpu.roll(sums[0], 96, 1), sums[1] + pltpu.roll(sums[1], 32, 1)]
            pool[r, 128 * i : 128 * i + 128] = (0.25 * jnp.where(even, sums[0], sums[1])).astype(BF)

    loop(wh + 6, c2, second)
    clear(a2, four, 3)
    clear(pool, [()], 3)

    def third(dj, off, size):
        x = jnp.concatenate([pool[rows(-2 + k, off, size), :] for k in (-1, 0, 1)], axis=1)
        y = relu(dot(x, t3[...]))
        for h in range(2):
            m1[h, rows(-2, off, size), :] = y[:, 256 * h : 256 * h + 256]

    loop(wh + 4, (wh + 4) // 2, third)
    clear(m1, both, 2)

    def fourth(dj, off, size):
        for h in range(2):
            other = slice(0, 64) if h == 0 else slice(192, 256)
            own = [m1[h, rows(-1 + k, off, size), :] for k in (-1, 0, 1)]
            edge = [m1[1 - h, rows(-1 + k, off, size), other] for k in (-1, 0, 1)]
            m2[h, rows(-1, off, size), :] = relu(dot(jnp.concatenate(own + edge, axis=1), t4[h]))

    loop(wh + 2, (wh + 2) // 2, fourth)
    clear(m2, both, 1)

    def fifth(dj, off, size):
        for q, h in four:
            j0 = -q
            other = slice(0, 32) if h == 0 else slice(224, 256)
            own = [a2[qs, h, rows(j0 + k, off, size), :] for qs, k in near(q)]
            edge = [a2[qs, 1 - h, rows(j0 + k, off, size), other] for qs, k in near(q)]
            other = slice(0, 64) if h == 0 else slice(192, 256)
            cells = (-1, 0) if q == 0 else (0, 1)
            own += [m2[h, rows(j0 + k, off, size), :] for k in cells]
            edge += [m2[1 - h, rows(j0 + k, off, size), other] for k in cells]
            d1[q, h, rows(j0, off, size), :] = relu(dot(jnp.concatenate(own + edge, axis=1), t5[q, h]))

    loop(wh + 1, {9: 3, 33: 11}[wh + 1], fifth)
    clear(d1, four, 1)

    def sixth(dj, off, size):
        outs = fine_conv(d1, t6, 0, off, size)
        for q in range(2):
            x = jnp.concatenate(outs[q, 0] + outs[q, 1], axis=1)
            emit(q, dj, c6, dot(x, th[...]))

    loop(wh, c6, sixth)


def unet_scratch(n, wh):
    m = (wh + 8) * n
    return [
        pltpu.VMEM((2, m, 16), BF),
        pltpu.VMEM((2, m, 128), BF),
        pltpu.VMEM((2, 2, m, 256), BF),
        pltpu.VMEM((2, 2, m, 256), BF),
        pltpu.VMEM((m, 256), BF),
        pltpu.VMEM((2, m, 256), BF),
        pltpu.VMEM((2, m, 256), BF),
        pltpu.VMEM((2, 2, m, 256), BF),
    ]


def xz_kernel(edges, v, *refs):
    held, out, tables, (vf, pf, hx), join, scratch = refs[0], refs[1], refs[2:6], refs[6:9], refs[9:12], refs[12:]
    weights = (*tables, *join)
    n, wh = 16, 32
    for z in range(16):
        vf[16 * z : 16 * z + 16, :] = v[z].astype(F32)
    for y in range(16):
        turned = jnp.transpose(vf[pl.ds(y, 16, stride=16), :])
        pf[pl.ds(y, 80, stride=16), 0:16] = turned[0:80, :]
    p = scratch[0]
    for x in range(80):
        p[x % 2, 16 * (x // 2) : 16 * (x // 2) + 16, :] = pf[16 * x : 16 * x + 16, 0:16].astype(BF)

    build_tables(held, *tables)
    build_join(held, *join)

    def emit(q, j0, cols, head):
        for k in range(cols):
            at = pl.multiple_of((2 * (j0 + k) + q) * n, 16)
            hx[pl.ds(at, n), :] = head[k * n : k * n + n, :]

    network(edges, n, wh, *scratch, weights, emit)
    for y in range(16):
        out[y] = jnp.transpose(hx[pl.ds(y, 64, stride=16), :])[0:16, :]


def spread_kernel(place, v, row, out):
    t = place[0]
    lane = iota((16, 128), 1)
    pairs = []
    for z in range(8):
        low = pltpu.roll(v[z].astype(F32), 128 - HALO, 1)
        high = pltpu.roll(v[z + 8].astype(F32), 64 - HALO, 1)
        pairs.append(jnp.where(lane < 64, low, high))
    last = [jnp.concatenate([pairs[2 * k][8:], pairs[2 * k + 1][8:]], axis=0).astype(BF) for k in range(4)]
    first = [jnp.concatenate([pairs[2 * k][:8], pairs[2 * k + 1][:8]], axis=0).astype(BF) for k in range(4)]
    for p in range(16):
        for rows, cond in ((last, t < p), (first, t >= p)):

            @pl.when(cond)
            def _(p=p, rows=rows):
                for k in range(4):
                    out[p, k] = rows[k]

        out[p, 4] = row[...]


def yz_kernel(edges, v, shared, xz, *refs):
    tables, held, (out, vf, hf, hy, rf, vc, hc, oc), join, scratch = refs[:4], refs[4], refs[5:13], refs[13:16], refs[16:]
    weights = (*tables, *join)
    build_join(held, *join)
    wh = 8
    p = scratch[0]
    tile, octet = edges[2], 8 * edges[3]
    for z in range(16):
        vf[16 * z : 16 * z + 16, :] = v[z].astype(F32)
    for side, source in ((0, jnp.maximum(tile - 1, 0)), (1, jnp.minimum(tile + 1, 15))):
        for k in range(4):
            both = shared[source, k].astype(F32)
            for i in range(2):
                at = 16 * (2 * k + i) + 8 * side
                hf[at : at + 8, :] = both[8 * i : 8 * i + 8, :]

    flags = sum(shared[octet + i, 4].astype(F32) for i in range(8))
    square = (128, 128)
    earlier = (iota(square, 0) < iota(square, 1)).astype(F32).astype(BF)
    rank = dot(flags.astype(BF), earlier)[0:1].astype(jnp.int32)
    yes = flags[0:1] > 0.5
    spots = jnp.where((iota(square, 0) == rank) & yes, 1.0, 0.0)
    back = jnp.transpose(spots)
    twice = back + pltpu.roll(pltpu.roll(back, 64, 0), 64, 1)
    vc[...] = dot(vf[...].astype(BF), pltpu.roll(back, HALO, 0).astype(BF))
    hc[...] = dot(hf[...].astype(BF), twice.astype(BF))
    count = jnp.sum(flags[0:1]).astype(jnp.int32)
    oc[...] = jnp.zeros_like(oc)

    def run(n):
        for k in range(32):
            at = slice(n * (k // 2), n * (k // 2) + n)
            if 8 <= k < 24:
                turned = jnp.transpose(vc[pl.ds(k - 8, 16, stride=16), :])
                p[k % 2, at, :] = turned[0:n, :].astype(BF)
            else:
                turned = jnp.transpose(hc[pl.ds(k if k < 8 else k - 16, 8, stride=16), :])
                p[k % 2, at, :] = jnp.concatenate([turned[0:n, :], turned[64 : 64 + n, :]], axis=1).astype(BF)

        def emit(q, j0, cols, head):
            for k in range(cols):
                at = pl.multiple_of((2 * (j0 + k) + q) * n, 16)
                hy[pl.ds(at, n), :] = head[k * n : k * n + n, :]

        network(edges, n, wh, *scratch, weights, emit)
        for y in range(16):
            plane = vc[pl.ds(y, 16, stride=16), :][:, 0:n]
            new = plane + jnp.transpose(hy[n * y : n * y + n, :])[0:16, :]
            oc[16 * y : 16 * y + 16, 0:n] = new.astype(BF)

    for n, low in ((32, -1), (48, 32), (64, 48)):

        @pl.when((count > low) & (count <= (32 if low < 0 else low + 16)))
        def _(n=n):
            run(n)

    spread = dot(oc[...], spots.astype(BF))
    yes = yes[:, 0:64]
    for y in range(16):
        plane = pltpu.roll(vf[pl.ds(y, 16, stride=16), :], 128 - HALO, 1)[:, 0:64]
        yz = jnp.where(yes, spread[16 * y : 16 * y + 16, 0:64], plane)
        xz_new = (plane + xz[y]).astype(BF).astype(F32)
        xz_new = jnp.where(edges[4 + y] > 0, xz_new, plane)
        rf[pl.ds(y, 16, stride=16), 0:64] = 0.5 * (xz_new + yz)
    for z in range(16):
        block = rf[16 * z : 16 * z + 16, 0:64].astype(BF)
        out[2 * (z // 2), z % 2] = block
        out[2 * (z // 2) + 1, z % 2] = block


def pack_kernel(side, v, out):
    for c, shift in ((0, HALO), (1, 1024 + HALO - 64)):

        @pl.when(side[0] == c)
        def _(shift=shift):
            for z in range(2):
                rolled = pltpu.roll(v[z].astype(F32), shift, 1).astype(BF)
                for s in range(8):
                    out[s, z] = rolled[:, 128 * s : 128 * s + 128]


def compute(xz_edges, yz_edges, v, shared, raw):
    xz, *tables = pl.pallas_call(
        xz_kernel,
        out_shape=[jax.ShapeDtypeStruct((16, 16, 64), F32)] + [jax.ShapeDtypeStruct(s, BF) for s in TABLES],
        in_specs=[SMEM, VMEM, VMEM],
        out_specs=[VMEM] * 5,
        scratch_shapes=[pltpu.VMEM((256, 128), F32), pltpu.VMEM((1280, 128), F32), pltpu.VMEM((1024, 128), F32)]
        + [pltpu.VMEM(s, BF) for s in JOIN]
        + unet_scratch(16, 32),
        compiler_params=pltpu.CompilerParams(vmem_limit_bytes=24 << 20),
        cost_estimate=pl.CostEstimate(flops=6_000_000_000, bytes_accessed=6_000_000, transcendentals=0),
        name="xz",
    )(xz_edges, v, raw)
    return pl.pallas_call(
        yz_kernel,
        out_shape=jax.ShapeDtypeStruct((16, 2, 16, 64), BF),
        in_specs=[SMEM] + [VMEM] * 8,
        out_specs=VMEM,
        scratch_shapes=[
            pltpu.VMEM((256, 128), F32),
            pltpu.VMEM((128, 128), F32),
            pltpu.VMEM((1024, 128), F32),
            pltpu.VMEM((256, 128), F32),
            pltpu.VMEM((256, 128), F32),
            pltpu.VMEM((128, 128), F32),
            pltpu.VMEM((256, 128), BF),
        ]
        + [pltpu.VMEM(s, BF) for s in JOIN]
        + unet_scratch(64, 8),
        compiler_params=pltpu.CompilerParams(vmem_limit_bytes=24 << 20),
        cost_estimate=pl.CostEstimate(flops=6_000_000_000, bytes_accessed=6_000_000, transcendentals=0),
        name="yz",
    )(yz_edges, v, shared, xz, *tables, raw)


def per_device(volume, xz_tissue, yz_tissue, *weights):
    slab, tile, ch = lax.axis_index("slab"), lax.axis_index("tile"), lax.axis_index("ch")
    packed = pl.pallas_call(
        pack_kernel,
        out_shape=jax.ShapeDtypeStruct((8, 2, 16, 128), BF),
        in_specs=[SMEM, VMEM],
        out_specs=VMEM,
        name="pack",
    )(ch[None].astype(jnp.int32), volume)
    moved = lax.all_to_all(packed, "slab", split_axis=0, concat_axis=0, tiled=True)
    v = moved.reshape(16, 16, 128)
    raw = stage(prepare(*weights))

    mine = (jnp.arange(128) // 8 == tile % 8)[None, :]
    row = jnp.where(mine, jnp.tile(yz_tissue, 16)[None, :], 0).astype(BF)
    shared = pl.pallas_call(
        spread_kernel,
        out_shape=jax.ShapeDtypeStruct((16, 5, 16, 128), BF),
        in_specs=[SMEM, VMEM, VMEM],
        out_specs=VMEM,
        compiler_params=pltpu.CompilerParams(vmem_limit_bytes=8 << 20),
        name="spread",
    )(tile[None].astype(jnp.int32), v, jnp.broadcast_to(row, (16, 128)))
    shared = lax.all_to_all(shared, "tile", split_axis=0, concat_axis=0, tiled=True)

    window = 2 * slab + ch
    xz_edges = jnp.stack([window == 0, window == 15]).astype(jnp.int32)
    yz_edges = jnp.stack([tile == 0, tile == 15, tile, ch]).astype(jnp.int32)
    yz_edges = jnp.concatenate([yz_edges, xz_tissue])

    block = compute(xz_edges, yz_edges, v, shared, raw)
    back = lax.all_to_all(block, ("slab", "ch"), split_axis=0, concat_axis=0, tiled=True)
    return jnp.transpose(back, (1, 2, 0, 3)).reshape(2, 16, 1024)


def solution(mesh):
    return jax.shard_map(
        per_device,
        mesh=mesh,
        in_specs=(P("slab", "tile", None), P("tile"), P(("slab", "tile"))) + (P(),) * 7,
        out_specs=P("slab", "tile", None),
        check_vma=False,
    )
```
